32 devices in a mesh: fsdp: 8 (over z, x), dp: 4 (over y, core).
Axes of the slice: x: 2, y: 2, z: 4, core: 2. Of those that a mesh axis runs over, the one named last changes fastest.
Arguments:
- tokens: bfloat16 [4, 4096, 1024], P('dp', 'fsdp'), may hold values from -6 to 6
- cotangent: bfloat16 [4, 4096, 1024], P('dp', 'fsdp'), may hold values from -6 to 6
- lengths: int32 [4, 32], P('dp'), may hold values from 8 to 248, as said below
- dealing: int32 [4, 32], P('dp'), may hold values from 0 to 31, as said below
- gain_mix: bfloat16 [1024], P('fsdp'), may hold values from 0.099609375 to 1.8984375
- w_qkv: bfloat16 [1024, 4096], P('fsdp'), may hold values from -0.1875 to 0.1875
- w_gates: bfloat16 [1024, 16], P('fsdp'), may hold values from -0.1875 to 0.1875
- w_outgate: bfloat16 [1024, 2048], P('fsdp'), may hold values from -0.1875 to 0.1875
- conv_weight: bfloat16 [4096, 4], P('fsdp'), may hold values from -3 to 3
- a_log: float32 [8], replicated, may hold values from -6 to -2
- dt_bias: float32 [8], replicated, may hold values from -2 to 2
- out_norm_gain: float32 [256], replicated, may hold values from 0.1 to 1.9
- w_out: bfloat16 [2048, 1024], P('fsdp'), may hold values from -0.125 to 0.125
- gain_ffn: bfloat16 [1024], P('fsdp'), may hold values from 0.099609375 to 1.8984375
- w_gate: bfloat16 [1024, 2816], P('fsdp'), may hold values from -0.1875 to 0.1875
- w_up: bfloat16 [1024, 2816], P('fsdp'), may hold values from -0.1875 to 0.1875
- w_down: bfloat16 [2816, 1024], P('fsdp'), may hold values from -0.109375 to 0.109375
Outputs:
- output: bfloat16 [4, 4096, 1024], P('dp', 'fsdp')
- input_grad: bfloat16 [4, 4096, 1024], P('dp', 'fsdp')
- grad_gain_mix: float32 [1024], P('fsdp')
- grad_qkv: float32 [1024, 4096], P('fsdp')
- grad_gates: float32 [1024, 16], P('fsdp')
- grad_outgate: float32 [1024, 2048], P('fsdp')
- grad_conv: float32 [4096, 4], P('fsdp')
- grad_a_log: float32 [8], replicated
- grad_dt_bias: float32 [8], replicated
- grad_out_norm: float32 [256], replicated
- grad_out: float32 [2048, 1024], P('fsdp')
- grad_gain_ffn: float32 [1024], P('fsdp')
- grad_gate: float32 [1024, 2816], P('fsdp')
- grad_up: float32 [1024, 2816], P('fsdp')
- grad_down: float32 [2816, 1024], P('fsdp')
The draws below stay inside these ranges and needn't reach their ends.
Inputs may be any that keep to these rules, and one draw needn't show every extreme that they name: Every length is a multiple of 8, and the 2 sequences dealt to one slot group (one device and micro-batch) have lengths that sum to 256. In each replica a permutation of 0 to 31: sequence k of the given order goes to slot p = dealing[k], that is to fsdp device p // 4, micro-batch (p // 2) % 2, place p % 2 there.
All inputs are finite; a program needn't handle non-finite values.
Results may differ from the reference program's by a relative error of at most 0.014.
Values may be sent and summed in bfloat16 or wider, within the bound.
No kernel may reach another device: no remote copies, remote signals or barrier semaphores. Data moves between devices by JAX's collectives and lax.ppermute only.
A program may use at most 384 MiB of HBM per device.

```python
import jax
import jax.numpy as jnp
from jax import lax

D = 1024
H = 8
DK = 128
DV = 256
CONV = 4
FF = 2816
SPAN = 64
MB_TOK = 256
MICRO = 2
SEQ_MB = 2
QKV = 4096
VW = 2048
SHARDS = 8
REPLICAS = 4
TOK_DEV = 512
TOK_GROUP = 4096
SEQS = 32
N_FSDP = 8
N_DP = 4


def deal_plan(key):
    units = MB_TOK // SHARDS
    blocks = SHARDS * MICRO
    first = jax.random.randint(jax.random.fold_in(key, 5), (REPLICAS, blocks), 1, units)
    column = jnp.arange(blocks, dtype=jnp.int32)[None, :]
    first = jnp.where(column == 0, units - 1, first).astype(jnp.int32)
    dealt = jnp.stack([first, units - first], axis=2).reshape(REPLICAS, SEQS) * SHARDS
    keys = jax.random.split(jax.random.fold_in(key, 9), REPLICAS)
    order = jax.vmap(lambda single: jax.random.permutation(single, SEQS))(keys).astype(jnp.int32)
    seq_len = jnp.take_along_axis(dealt, order, axis=1)
    return (seq_len.astype(jnp.int32), order)


def draw_lengths(key, part):
    return deal_plan(key)[0]


def draw_dealing(key, part):
    return deal_plan(key)[1]


def steps_of(rng, shape, shards, smallest, high):
    def one(dim, blocks):
        steps = jax.random.uniform(jax.random.fold_in(jax.random.fold_in(rng, 6), dim), (blocks,), jnp.float32, smallest / len(shards), high / len(shards))
        return jnp.repeat(jnp.exp(steps), shape[dim] // blocks).reshape((-1,) + (1,) * (len(shape) - dim - 1))

    level = one(*shards[0])
    for cut in shards[1:]:
        level = level * one(*cut)
    return level


def noise(key, shape, scale, reach, cuts=(), kind=jnp.bfloat16):
    values = jax.random.normal(key, shape, jnp.float32) * scale
    if len(cuts) > 0:
        values = steps_of(key, shape, cuts, -0.22, 0.18) * values
    return jnp.clip(values, min=-reach, max=reach).astype(kind)


def setup_inputs(seed: int = 0) -> dict:
    key_of = jax.random.split(jax.random.key(seed), 18)
    return {
        "tokens": noise(key_of[0], (REPLICAS, TOK_GROUP, D), 1.0, 6.0, ((0, 4), (1, 8))),
        "cotangent": noise(key_of[1], (REPLICAS, TOK_GROUP, D), 1.0, 6.0, ((0, 4), (1, 8))),
        "lengths": draw_lengths(jax.random.fold_in(key_of[17], 71), 0),
        "dealing": draw_dealing(jax.random.fold_in(key_of[17], 71), 0),
        "gain_mix": jnp.clip(1.0 + 0.18 * jax.random.normal(key_of[4], (D,), jnp.float32), 0.099609375, 1.8984375).astype(jnp.bfloat16),
        "w_qkv": noise(key_of[5], (D, QKV), D ** -0.5, 0.1875, ((0, 8),)),
        "w_gates": noise(key_of[6], (D, 2 * H), D ** -0.5, 0.1875, ((0, 8),)),
        "w_outgate": noise(key_of[7], (D, VW), D ** -0.5, 0.1875, ((0, 8),)),
        "conv_weight": noise(key_of[8], (QKV, CONV), 0.5, 3.0, ((0, 8),)),
        "a_log": jnp.clip(jax.random.uniform(key_of[9], (H,), jnp.float32, -6.0, -2.0), -6.0, -2.0),
        "dt_bias": jnp.clip(jax.random.uniform(key_of[10], (H,), jnp.float32, -2.0, 2.0), -2.0, 2.0),
        "out_norm_gain": jnp.clip(1.0 + 0.18 * jax.random.normal(key_of[11], (DV,), jnp.float32), 0.1, 1.9),
        "w_out": noise(key_of[12], (VW, D), VW ** -0.5, 0.125, ((0, 8),)),
        "gain_ffn": jnp.clip(1.0 + 0.18 * jax.random.normal(key_of[13], (D,), jnp.float32), 0.099609375, 1.8984375).astype(jnp.bfloat16),
        "w_gate": noise(key_of[14], (D, FF), D ** -0.5, 0.1875, ((0, 8),)),
        "w_up": noise(key_of[15], (D, FF), D ** -0.5, 0.1875, ((0, 8),)),
        "w_down": noise(key_of[16], (FF, D), FF ** -0.5, 0.109375, ((0, 8),)),
    }


@jax.custom_vjp
def low(v):
    return lax.optimization_barrier(v.astype(jnp.bfloat16)).astype(jnp.float32)

@jax.custom_vjp
def low_back(v):
    return v

def low_keep(v):
    return (low(v), None)

def low_pass(kept, grad):
    return (grad,)

def back_keep(v):
    return (v, None)

def back_low(kept, grad):
    return (low(grad),)
low.defvjp(low_keep, low_pass)
low_back.defvjp(back_keep, back_low)
norm_eps = 1e-05
unit_eps = 1e-06
highest = lax.Precision.HIGHEST

def matmul(left, right):
    return jnp.dot(left, right, preferred_element_type=jnp.float32, precision=highest)

def rms_scale(values, gain):
    return values * lax.rsqrt(lax.optimization_barrier(jnp.mean(values * values, axis=-1, keepdims=True)) + norm_eps) * gain

def causal_conv(signal, weight, position):
    taps = weight.shape[1]
    rows = signal.shape[0]
    padded = jnp.concatenate([jnp.zeros((taps - 1, signal.shape[1]), signal.dtype), signal], axis=0)
    total = jnp.zeros_like(signal)
    for offset in range(taps):
        delay = taps - 1 - offset
        shifted = padded[offset:offset + rows]
        total = total + jnp.where((position >= delay)[:, None], shifted, 0.0) * weight[:, offset]
    return total

def mixer_inputs(projected, gate_in, conv_weight, a_log, dt_bias, position):
    rows = projected.shape[0]
    mixed = jax.nn.silu(causal_conv(projected, conv_weight, position))
    queries = mixed[:, :H * DK].reshape(rows, H, DK)
    keys = mixed[:, H * DK:2 * H * DK].reshape(rows, H, DK)
    values = mixed[:, 2 * H * DK:].reshape(rows, H, DV)
    queries = queries * lax.rsqrt(lax.optimization_barrier(jnp.sum(queries * queries, axis=-1, keepdims=True)) + unit_eps) * DK ** (-0.5)
    keys = keys * lax.rsqrt(lax.optimization_barrier(jnp.sum(keys * keys, axis=-1, keepdims=True)) + unit_eps)
    decay = -jnp.exp(a_log) * jax.nn.softplus(gate_in[:, :H] + dt_bias)
    strength = jax.nn.sigmoid(gate_in[:, H:])
    return (queries, keys, values, decay, strength)

def output_norm(heads_out, out_gate, out_gain):
    rows = heads_out.shape[0]
    scaled = heads_out * lax.rsqrt(lax.optimization_barrier(jnp.mean(heads_out * heads_out, axis=-1, keepdims=True)) + norm_eps) * out_gain
    return scaled.reshape(rows, H * DV) * jax.nn.silu(out_gate)

def delta_tokens(queries, keys, values, decay, strength, position):
    begin = (position == 0).astype(queries.dtype)

    def one_token(state, inputs):
        query, key, value, rate, beta, first = inputs
        kept = state * (jnp.exp(rate) * (1.0 - first))[:, None, None]
        recalled = jnp.einsum('hd,hde->he', key, kept, precision=highest)
        state = kept + jnp.einsum('hd,he->hde', key, (value - recalled) * beta[:, None], precision=highest)
        return (state, jnp.einsum('hd,hde->he', query, state, precision=highest))

    @jax.checkpoint
    def one_block(state, inputs):
        return lax.scan(one_token, state, inputs)
    rows = queries.shape[0]

    def blocks(array):
        return array.reshape((rows // SPAN, SPAN) + array.shape[1:])
    stacked = tuple((blocks(item) for item in (queries, keys, values, decay, strength, begin)))
    start = jnp.zeros((H, DK, DV), queries.dtype)
    final, outputs = lax.scan(one_block, start, stacked)
    return outputs.reshape(rows, H, DV)

def block_forward(inputs, params, position):
    gain_mix, w_qkv, w_gates, w_outgate, conv_weight, a_log, dt_bias, out_gain, w_out, gain_ffn, w_gate, w_up, w_down = params
    normed = low(rms_scale(inputs, gain_mix))
    projected = low_back(matmul(normed, w_qkv))
    gate_in = low_back(matmul(normed, w_gates))
    out_gate = low_back(matmul(normed, w_outgate))
    queries, keys, values, decay, strength = mixer_inputs(projected, gate_in, conv_weight, a_log, dt_bias, position)
    heads_out = delta_tokens(queries, keys, values, decay, strength, position)
    gated = low(output_norm(heads_out, out_gate, out_gain))
    residual = inputs + low_back(matmul(gated, w_out))
    normed_ffn = low(rms_scale(residual, gain_ffn))
    gate_act = low_back(matmul(normed_ffn, w_gate))
    up_act = low_back(matmul(normed_ffn, w_up))
    hidden = low(jax.nn.silu(gate_act) * up_act)
    return residual + low_back(matmul(hidden, w_down))

def dealt_layout(seq_len, dealt_slot):
    piece = seq_len // N_FSDP
    begin_given = jnp.cumsum(piece) - piece
    holder = jnp.argsort(dealt_slot).astype(jnp.int32)
    slot_len = seq_len[holder].reshape(N_FSDP * MICRO, SEQ_MB)
    slot_piece = piece[holder].reshape(N_FSDP * MICRO, SEQ_MB)
    slot_given = begin_given[holder].reshape(N_FSDP * MICRO, SEQ_MB)
    slot_start = jnp.cumsum(slot_len, axis=1) - slot_len
    place = jnp.arange(MB_TOK, dtype=jnp.int32)
    offset = place[None, :, None] - slot_start[:, None, :]
    inside = (offset >= 0) & (offset < slot_len[:, None, :])
    source = offset // slot_piece[:, None, :]
    row = source * TOK_DEV + slot_given[:, None, :] + offset % slot_piece[:, None, :]
    index = lax.optimization_barrier(jnp.sum(jnp.where(inside, row, 0), axis=2)).astype(jnp.int32)
    position = lax.optimization_barrier(jnp.sum(jnp.where(inside, offset, 0), axis=2)).astype(jnp.int32)
    return (index, position)

def reference(tokens, cotangent, lengths, dealing, gain_mix, w_qkv, w_gates, w_outgate, conv_weight, a_log, dt_bias, out_norm_gain, w_out, gain_ffn, w_gate, w_up, w_down):
    params = tuple((item.astype(jnp.float32) for item in (gain_mix, w_qkv, w_gates, w_outgate, conv_weight, a_log, dt_bias, out_norm_gain, w_out, gain_ffn, w_gate, w_up, w_down)))
    index, position = jax.vmap(dealt_layout)(lengths, dealing)
    replica = (jnp.arange(N_DP, dtype=jnp.int32) * TOK_GROUP)[:, None, None]
    flat_index = (index + replica).reshape(-1, MB_TOK)
    flat_place = position.reshape(-1, MB_TOK)
    width = tokens.shape[2]
    flat_tokens = tokens.reshape(-1, width).astype(jnp.float32)
    flat_cot = cotangent.reshape(-1, width).astype(jnp.float32)

    def one_block(totals, inputs):
        rows, place = inputs
        result, back = jax.vjp(lambda block_rows, weights: block_forward(block_rows, weights, place), flat_tokens[rows], params)
        grad_in, grad_weights = back(flat_cot[rows])
        totals = jax.tree.map(jnp.add, totals, grad_weights)
        return (totals, (result, grad_in))
    zeros = jax.tree.map(jnp.zeros_like, params)
    totals, (results, grads_in) = lax.scan(one_block, zeros, (flat_index, flat_place))
    where_rows = flat_index.reshape(-1)
    output = jnp.zeros_like(flat_tokens).at[where_rows].set(results.reshape(-1, width))
    input_grad = jnp.zeros_like(flat_tokens).at[where_rows].set(grads_in.reshape(-1, width))
    output = output.reshape(tokens.shape).astype(jnp.bfloat16)
    input_grad = input_grad.reshape(tokens.shape).astype(jnp.bfloat16)
    return (output, input_grad, totals[0], totals[1], totals[2], totals[3], totals[4], totals[5], totals[6], totals[7], totals[8], totals[9], totals[10], totals[11], totals[12])
```

```python
from functools import partial

import jax
import jax.numpy as jnp
from jax import lax
from jax.experimental import pallas as pl
from jax.experimental.pallas import tpu as pltpu
from jax.sharding import PartitionSpec as P

H = 8
DK = 128
DV = 256
TAPS = 4
MB_TOK = 256
MICRO = 2
SEQ_MB = 2
ROWS = MB_TOK * MICRO

norm_eps = 1e-05
unit_eps = 1e-06
f32 = jnp.float32
bf16 = jnp.bfloat16
NN = (((1,), (0,)), ((), ()))
NT = (((1,), (1,)), ((), ()))
TN = (((0,), (0,)), ((), ()))


def mm(left, right, dims=NN):
    return lax.dot_general(
        left.astype(bf16), right.astype(bf16), dims, preferred_element_type=f32
    )


def halves(value):
    high = value.astype(bf16)
    return high, (value - high.astype(f32)).astype(bf16)


def mm_split(left, right, dims=NN):
    return mm(left[0], right[0], dims) + (mm(left[0], right[1], dims) + mm(left[1], right[0], dims))


def conv_taps(signal, weight, position):
    total = signal * weight[TAPS - 1 : TAPS]
    shifted = []
    for delay in range(1, TAPS):
        moved = jnp.where(position >= delay, pltpu.roll(signal, delay, 0), 0.0)
        shifted.append(moved)
        total = total + moved * weight[TAPS - 1 - delay : TAPS - delay]
    return total, shifted


def unit_rows(value):
    return lax.rsqrt(jnp.sum(value * value, axis=1, keepdims=True) + unit_eps)


def chain_masks(label_col, label_row):
    size = MB_TOK
    row = lax.broadcasted_iota(jnp.int32, (size, size), 0)
    col = lax.broadcasted_iota(jnp.int32, (size, size), 1)
    same = label_col == label_row
    return row, col, (row >= col) & same, (row > col) & same


def unit_lower_inverses(systems):
    row = lax.broadcasted_iota(jnp.int32, (MB_TOK, MB_TOK), 0)
    col = lax.broadcasted_iota(jnp.int32, (MB_TOK, MB_TOK), 1)
    apart = row ^ col
    eye = jnp.where(row == col, 1.0, 0.0)
    inverses = [eye - jnp.where(apart == 1, system, 0.0) for system in systems]
    lows = [system.astype(bf16) for system in systems]
    level = 1
    while (1 << level) < MB_TOK:
        now = (apart >> level) == 1
        pairs = [inverse.astype(bf16) for inverse in inverses]
        halfway = [mm(pair, jnp.where(now, low, 0)) for pair, low in zip(pairs, lows)]
        inverses = [
            inverse - mm(half, pair) for inverse, half, pair in zip(inverses, halfway, pairs)
        ]
        level += 1
    pairs = [halves(inverse) for inverse in inverses]
    rests = [
        eye - inverse - mm_split(halves(system), pair)
        for inverse, system, pair in zip(inverses, systems, pairs)
    ]
    return [inverse + mm(pair[0], rest) for inverse, pair, rest in zip(inverses, pairs, rests)]


def mixer_forward_kernel(
    pq, pk, pv, og, col, row, wq, wk, wv, gain, gated_ref, inverse_ref, pseudo_ref
):
    position = col[0, :, 3:4]
    query, key, value = (
        pre * jax.nn.sigmoid(pre)
        for pre in (
            conv_taps(pq[...], wq[...], position)[0],
            conv_taps(pk[...], wk[...], position)[0],
            conv_taps(pv[...], wv[...], position)[0],
        )
    )
    query = (query * (unit_rows(query) * DK ** (-0.5))).astype(bf16)
    key = (key * unit_rows(key)).astype(bf16)
    chains = [slice(chain * MB_TOK, (chain + 1) * MB_TOK) for chain in range(MICRO)]
    systems, attends = [], []
    for rows in chains:
        _, _, lower, strict = chain_masks(col[0, rows, 2:3], row[0, 2:3, rows])
        spread = jnp.where(lower, col[0, rows, 0:1] - row[0, 0:1, rows], 0.0)
        weight = jnp.exp(spread) * row[0, 1:2, rows]
        systems.append(jnp.where(strict, weight * mm(key[rows], key[rows], NT), 0.0))
        attends.append(jnp.where(lower, weight * mm(query[rows], key[rows], NT), 0.0).astype(bf16))
    inverses = unit_lower_inverses(systems)
    for rows, inverse, attend in zip(chains, inverses, attends):
        low = inverse.astype(bf16)
        inverse_ref[0, rows] = low
        pseudo = mm(low, value[rows]).astype(bf16)
        pseudo_ref[0, rows] = pseudo
        heads_out = mm(attend, pseudo)
        scale = lax.rsqrt(jnp.mean(heads_out * heads_out, axis=1, keepdims=True) + norm_eps)
        gate = og[rows]
        gated_ref[rows] = (
            heads_out * scale * gain[...] * (gate * jax.nn.sigmoid(gate))
        ).astype(bf16)


def silu_back(pre, sig):
    return sig * (1.0 + pre * (1.0 - sig))


def conv_back(grad, shifted, signal, weight, position):
    out = grad * weight[TAPS - 1 : TAPS]
    taps = [jnp.sum(grad * signal, axis=0, keepdims=True)]
    for delay in range(1, TAPS):
        taps.append(jnp.sum(grad * shifted[delay - 1], axis=0, keepdims=True))
        kept = jnp.where(position >= delay, grad, 0.0)
        out = out + pltpu.roll(kept, ROWS - delay, 0) * weight[TAPS - 1 - delay : TAPS - delay]
    return out, jnp.concatenate(taps[::-1], axis=0)


def mixer_backward_kernel(
    pq, pk, pv, og, gg, col, row, wq, wk, wv, gain, inverse_ref, pseudo_ref,
    dq_ref, dk_ref, dv_ref, dog_ref, dwq_ref, dwk_ref, dwv_ref, dgain_ref, dcol_ref, drow_ref,
    gq_s, gk_s, gv_s,
):
    position = col[0, :, 3:4]
    pres = []
    for signal, weight in ((pq, wq), (pk, wk), (pv, wv)):
        pre, shifted = conv_taps(signal[...], weight[...], position)
        pres.append((pre, jax.nn.sigmoid(pre), shifted))
    mixed_q, mixed_k, value = (pre * sig for pre, sig, _ in pres)
    unit_q, unit_k = unit_rows(mixed_q), unit_rows(mixed_k)
    query = mixed_q * (unit_q * DK ** (-0.5))
    key = mixed_k * unit_k
    gain_total = jnp.zeros((1, DV), f32)
    for chain in range(MICRO):
        rows = slice(chain * MB_TOK, (chain + 1) * MB_TOK)
        at, to, lower, strict = chain_masks(col[0, rows, 2:3], row[0, 2:3, rows])
        spread = jnp.where(lower, col[0, rows, 0:1] - row[0, 0:1, rows], 0.0)
        fade = jnp.where(lower, jnp.exp(spread), 0.0)
        beta = row[0, 1:2, rows]
        q, k = query[rows].astype(bf16), key[rows].astype(bf16)
        system = jnp.where(strict, fade, 0.0) * mm(k, k, NT)
        attend = fade * mm(q, k, NT)
        spread_attend = (attend * beta).astype(bf16)
        pseudo_low = pseudo_ref[0, rows]
        heads_out = mm(spread_attend, pseudo_low)
        scale = lax.rsqrt(jnp.mean(heads_out * heads_out, axis=1, keepdims=True) + norm_eps)
        gate = og[rows]
        sig = jax.nn.sigmoid(gate)
        grad = gg[rows]
        unit = heads_out * scale
        dog_ref[rows] = (grad * unit * gain[...] * silu_back(gate, sig)).astype(bf16)
        grad = grad * (gate * sig)
        gain_total = gain_total + jnp.sum(grad * unit, axis=0, keepdims=True)
        grad = grad * gain[...]
        grad_out = scale * (grad - unit * jnp.mean(grad * unit, axis=1, keepdims=True))
        out_low = grad_out.astype(bf16)
        grad_attend = mm(out_low, pseudo_low, NT)
        grad_value = mm(inverse_ref[0, rows], mm(spread_attend, out_low, TN), TN)
        grad_system = -mm(grad_value, pseudo_low, NT)
        both = grad_attend * attend + grad_system * system
        drow_ref[0, 0:1, rows] = jnp.sum(both, axis=0, keepdims=True)
        dcol_ref[0, rows] = jnp.broadcast_to(
            jnp.sum(both * beta, axis=1, keepdims=True), (MB_TOK, 8)
        )
        weight = fade * beta
        from_attend = (grad_attend * weight).astype(bf16)
        from_system = (jnp.where(strict, grad_system, 0.0) * weight).astype(bf16)
        gq_s[rows] = mm(from_attend, k)
        gk_s[rows] = mm(from_attend, q, TN) + (mm(from_system, k) + mm(from_system, k, TN))
        gv_s[rows] = grad_value
    drow_ref[0, 1:8] = jnp.zeros((7, ROWS), f32)
    dgain_ref[0] = jnp.broadcast_to(gain_total, (8, DV))
    grad_q = gq_s[...] * DK ** (-0.5)
    unit = mixed_q * unit_q
    grad_q = unit_q * (grad_q - unit * jnp.sum(grad_q * unit, axis=1, keepdims=True))
    grad_k = gk_s[...]
    grad_k = unit_k * (grad_k - key * jnp.sum(grad_k * key, axis=1, keepdims=True))
    for grad, (pre, sig, shifted), signal, weight, out, dw in (
        (grad_q, pres[0], pq, wq, dq_ref, dwq_ref),
        (grad_k, pres[1], pk, wk, dk_ref, dwk_ref),
        (gv_s[...], pres[2], pv, wv, dv_ref, dwv_ref),
    ):
        back, taps = conv_back(
            grad * silu_back(pre, sig), shifted, signal[...], weight[...], position
        )
        out[...] = back.astype(bf16)
        dw[...] = taps


def columns(width, start):
    return pl.BlockSpec((ROWS, width), lambda head: (0, head + start))


def tap_columns(width, start):
    return pl.BlockSpec((TAPS, width), lambda head: (0, head + start))


def per_head(*shape, start=0):
    return pl.BlockSpec((1,) + shape, lambda head: (head + start,) + (0,) * len(shape))


def mixer_inputs(first):
    return (
        [columns(DK, first), columns(DK, H + first), columns(DV, H + first)]
        + [columns(DV, 2 * H + first)],
        [per_head(ROWS, 8, start=first), per_head(8, ROWS, start=first)]
        + [tap_columns(DK, first), tap_columns(DK, H + first), tap_columns(DV, H + first)]
        + [pl.BlockSpec((1, DV), lambda head: (0, 0))],
    )


def mixer_forward(projected, col, row, taps, gain, first, count):
    start, rest = mixer_inputs(first)
    return pl.pallas_call(
        mixer_forward_kernel,
        grid=(count,),
        in_specs=start + rest,
        out_specs=[columns(DV, 0), per_head(ROWS, MB_TOK), per_head(ROWS, DV)],
        out_shape=[
            jax.ShapeDtypeStruct((ROWS, count * DV), bf16),
            jax.ShapeDtypeStruct((count, ROWS, MB_TOK), bf16),
            jax.ShapeDtypeStruct((count, ROWS, DV), bf16),
        ],
        name="mixer_forward",
        cost_estimate=cost(4.4 * count),
    )(projected, projected, projected, projected, col, row, taps, taps, taps, gain)


def mixer_backward(projected, grad_gated, col, row, taps, gain, inverse, pseudo, first):
    start, rest = mixer_inputs(first)
    count = inverse.shape[0]
    return pl.pallas_call(
        mixer_backward_kernel,
        grid=(count,),
        in_specs=start
        + [columns(DV, first)]
        + rest
        + [per_head(ROWS, MB_TOK), per_head(ROWS, DV)],
        out_specs=[columns(DK, 0), columns(DK, 0), columns(DV, 0), columns(DV, 0)]
        + [tap_columns(DK, 0), tap_columns(DK, 0), tap_columns(DV, 0)]
        + [per_head(8, DV), per_head(ROWS, 8), per_head(8, ROWS)],
        out_shape=[
            jax.ShapeDtypeStruct((ROWS, count * DK), bf16),
            jax.ShapeDtypeStruct((ROWS, count * DK), bf16),
            jax.ShapeDtypeStruct((ROWS, count * DV), bf16),
            jax.ShapeDtypeStruct((ROWS, count * DV), bf16),
            jax.ShapeDtypeStruct((TAPS, count * DK), f32),
            jax.ShapeDtypeStruct((TAPS, count * DK), f32),
            jax.ShapeDtypeStruct((TAPS, count * DV), f32),
            jax.ShapeDtypeStruct((count, 8, DV), f32),
            jax.ShapeDtypeStruct((count, ROWS, 8), f32),
            jax.ShapeDtypeStruct((count, 8, ROWS), f32),
        ],
        scratch_shapes=[
            pltpu.VMEM((ROWS, DK), f32),
            pltpu.VMEM((ROWS, DK), f32),
            pltpu.VMEM((ROWS, DV), f32),
        ],
        name="mixer_backward",
        cost_estimate=cost(4.6 * count),
    )(
        projected, projected, projected, projected, grad_gated, col, row,
        taps, taps, taps, gain, inverse, pseudo,
    )


BLOCKS = tuple((dz, dx) for dx in (1, 0) for dz in (1, 3, 0, 2))


class Plane:
    def __init__(self):
        fsdp, dp = lax.axis_index("fsdp"), lax.axis_index("dp")
        self.z, self.x = fsdp // 2, fsdp % 2
        self.y, self.core = dp // 2, dp % 2

    @staticmethod
    def move(value, dz=0, dx=0, dy=0, dc=0):
        flip = (dz * 2 + dx) * 4 + dy * 2 + dc
        return lax.ppermute(value, ("fsdp", "dp"), [(here, here ^ flip) for here in range(32)])

    def units(self):
        own, other = [], []
        for dz, dx in BLOCKS:
            base = ((self.z ^ dz) * 2 + (self.x ^ dx)) * 2
            own.append(base + self.core)
            other.append(base + 1 - self.core)
        return jnp.stack(own + other).astype(jnp.int32)

    def half(self, shard):
        rows = shard.shape[0] // 2
        return lax.dynamic_slice_in_dim(shard, self.core * rows, rows, 0)

    def gather_small(self, row):
        fsdp = self.z * 2 + self.x
        rows = [row]
        for step in range(1, 8):
            pairs = [(i, (i // 4 ^ step) * 4 + i % 4) for i in range(32)]
            rows.append(lax.ppermute(row, ("fsdp", "dp"), pairs))
        place = jnp.arange(8, dtype=jnp.int32)
        picks = (place[:, None] ^ place[None, :]) == fsdp
        return exact(picks.astype(bf16), jnp.stack(rows).reshape(8, -1)).astype(bf16)

    def sum_small(self, value):
        for step in (1, 2, 4, 8, 16):
            value = value + lax.ppermute(value, ("fsdp", "dp"), [(i, i ^ step) for i in range(32)])
        return value


def after(value, *others):
    return lax.optimization_barrier((value,) + others)[0]


def summed(*terms):
    return sum(term.astype(f32) for term in terms).astype(bf16)


def gather_blocks(plane, half):
    got = {(0, 0): half, (1, 0): plane.move(half, dz=1), (2, 0): plane.move(half, dz=2)}
    got[3, 0] = plane.move(got[2, 0], dz=1)
    for dz in range(4):
        got[dz, 1] = plane.move(got[dz, 0], dx=1)
    return [got[at] for at in BLOCKS] + [plane.move(got[at], dc=1) for at in BLOCKS]


class Reduce:
    def __init__(self, plane, sums, split=False):
        self.plane, self.split = plane, split
        self.keep, self.send = sums
        self.back = plane.move(self.send, dc=1)

    def start(self, *others):
        back = after(self.back, *others)
        if not self.split:
            self.part = summed(self.keep[4:], back[4:])
            return self._beside(summed(self.keep[:4], back[:4]))

        def take(array, at):
            return lax.dynamic_slice_in_dim(array, at * 32, 32, 1)

        y = self.plane.y
        self.mine = summed(take(self.keep, y), take(back, y))
        sent = summed(take(self.keep, 1 - y), take(back, 1 - y))
        self.from_y = self.plane.move(sent, dy=1)
        return sent

    def _beside(self, sent):
        self.from_x = self.plane.move(sent, dx=1)
        return sent

    def beside(self, *others):
        from_y = after(self.from_y, *others)
        self.part = summed(self.mine[4:], from_y[4:])
        return self._beside(summed(self.mine[:4], from_y[:4]))

    def turn(self, *others):
        from_x = after(self.from_x, *others)
        sent = summed(self.part[:2], from_x[:2])
        self.rest = summed(self.part[2:], from_x[2:])
        self.from_z = self.plane.move(sent, dz=1)
        return sent

    def along(self, *others):
        self.near = after(self.from_z, *others)
        sent = summed(self.rest[1], self.near[1])
        self.far = self.plane.move(sent, dz=2)
        return sent

    def across(self, *others):
        self.total = summed(self.rest[0], self.near[0], after(self.far, *others))
        self.other = self.plane.move(self.total, dy=1)
        return self.total

    def close(self, *others):
        other = after(self.other, *others)
        if self.split:
            first = self.plane.y == 0
            total = jnp.concatenate(
                [jnp.where(first, self.total, other), jnp.where(first, other, self.total)], axis=0
            )
        else:
            total = summed(self.total, other)
        self.total, self.other = total, self.plane.move(total, dc=1)
        return total

    def halves(self):
        first = self.plane.core == 0
        return (
            jnp.where(first, self.total, self.other),
            jnp.where(first, self.other, self.total),
        )


def cost(us):
    return pl.CostEstimate(
        flops=int(us * 1.0e9), transcendentals=0, bytes_accessed=int(us * 3.0e6)
    )


def place(weight, units, blocks, rows, parts=1):
    width = weight.shape[1]
    for i, block in enumerate(blocks):
        for part in range(parts):
            count = min(rows - 64 * part, 64)
            start = pl.multiple_of(units[i] * rows + 64 * part, 16)
            weight[pl.ds(start, count), :] = block[:count, part * width : (part + 1) * width]


def project_kernel(units, x_ref, *refs):
    blocks, y_ref, weight = refs[:16], refs[16], refs[17]
    place(weight, units, blocks, 64)
    y_ref[...] = jnp.dot(x_ref[...], weight[...], preferred_element_type=f32)


def project(units, value, blocks, tile):
    width = blocks[0].shape[1]
    rows, depth = value.shape
    return pl.pallas_call(
        project_kernel,
        grid_spec=pltpu.PrefetchScalarGridSpec(
            num_scalar_prefetch=1,
            grid=(width // tile,),
            in_specs=[pl.BlockSpec((rows, depth), lambda n, s: (0, 0))]
            + [pl.BlockSpec((64, tile), lambda n, s: (0, n))] * 16,
            out_specs=pl.BlockSpec((rows, tile), lambda n, s: (0, n)),
            scratch_shapes=[pltpu.VMEM((depth, tile), bf16)],
        ),
        out_shape=jax.ShapeDtypeStruct((rows, width), f32),
        name="project",
        cost_estimate=cost(17),
    )(units, value, *blocks)


def tiles_of(arrays, tile):
    specs, firsts, first = [], [], 0
    for array in arrays:
        count = array.shape[1] // tile

        def index(n, s, first=first, count=count):
            return (0, jnp.clip(n - first, 0, count - 1))

        specs.append(pl.BlockSpec((array.shape[0], tile), index))
        firsts.append(first)
        first += count
    return specs, firsts, first


def pick(step, firsts, refs, chosen):
    for i, ref in enumerate(refs):
        here = step >= firsts[i]
        if i + 1 < len(refs):
            here = here & (step < firsts[i + 1])

        @pl.when(here)
        def _():
            chosen[...] = ref[...]


def back_project_kernel(firsts, units, *refs):
    rights, blocks = refs[: len(firsts)], refs[len(firsts) : len(firsts) + 16]
    out_ref, chosen, weight = refs[len(firsts) + 16 :]
    step = pl.program_id(0)
    pick(step, firsts, rights, chosen)
    place(weight, units, blocks, 64)
    part = lax.dot_general(chosen[...], weight[...], NT, preferred_element_type=f32)

    @pl.when(step == 0)
    def _():
        out_ref[...] = part

    @pl.when(step > 0)
    def _():
        out_ref[...] += part


def back_project(units, rights, blocks, depth, tile):
    specs, firsts, steps = tiles_of(rights, tile)
    rows = rights[0].shape[0]
    return pl.pallas_call(
        partial(back_project_kernel, tuple(firsts)),
        grid_spec=pltpu.PrefetchScalarGridSpec(
            num_scalar_prefetch=1,
            grid=(steps,),
            in_specs=specs + [pl.BlockSpec((64, tile), lambda n, s: (0, n))] * 16,
            out_specs=pl.BlockSpec((rows, depth), lambda n, s: (0, 0)),
            scratch_shapes=[pltpu.VMEM((rows, tile), bf16), pltpu.VMEM((depth, tile), bf16)],
        ),
        out_shape=jax.ShapeDtypeStruct((rows, depth), f32),
        name="back_project",
        cost_estimate=cost(18),
    )(units, *rights, *blocks)


def gram_kernel(firsts, rows, units, left_ref, *refs):
    rights = refs[: len(firsts)]
    keep, send, chosen, total = refs[-4:]
    step, part = pl.program_id(0), pl.program_id(1)

    @pl.when(part == 0)
    def _():
        pick(step, firsts, rights, chosen)
        total[0 : left_ref.shape[0], :] = jnp.dot(
            left_ref[...], chosen[...], preferred_element_type=f32
        )

    def block(i):
        value = total[pl.ds(pl.multiple_of(units[i] * rows + part * 64, 16), 64), :]
        if rows % 64:
            inside = lax.broadcasted_iota(jnp.int32, value.shape, 0) < rows - part * 64
            value = jnp.where(inside, value, 0.0)
        return value.astype(bf16)

    for i in range(8):
        keep[i] = block(i)
        send[i] = block(8 + i)


def gram_blocks(units, left, rights, tile, width, base=0, into=()):
    depth, inner = left.shape
    rows = depth // 16
    parts = -(-rows // 64)
    specs, firsts, steps = tiles_of(rights, tile)
    specs = [
        pl.BlockSpec(spec.block_shape, lambda n, p, s, index=spec.index_map: index(n, s))
        for spec in specs
    ]
    first = base // tile

    def column(n, p, s):
        return (0, first + p * steps + n)

    whole = pl.BlockSpec(memory_space=pl.ANY)
    out = pl.pallas_call(
        partial(gram_kernel, tuple(firsts), rows),
        grid_spec=pltpu.PrefetchScalarGridSpec(
            num_scalar_prefetch=1,
            grid=(steps, parts),
            in_specs=[pl.BlockSpec((depth, inner), lambda n, p, s: (0, 0))]
            + specs
            + [whole] * len(into),
            out_specs=[pl.BlockSpec((8, 64, tile), lambda n, p, s: (0,) + column(n, p, s))] * 2,
            scratch_shapes=[
                pltpu.VMEM((inner, tile), bf16),
                pltpu.VMEM((depth + 64, tile), f32),
            ],
        ),
        out_shape=[jax.ShapeDtypeStruct((8, 64, width), bf16)] * 2,
        input_output_aliases={2 + len(rights) + i: i for i in range(len(into))},
        name="gram_blocks",
        cost_estimate=cost(steps * tile * depth / 2.9e5),
    )(units, left, *rights, *into)
    return list(out)


FTILE = 256


PART = 32
DOWN_AT = (0, 96, 176, 256)


def late_quarter(w_down, w_out, w_gate, w_up):
    dp = lax.axis_index("dp")

    def parts(shard, start, rows):
        piece = lax.dynamic_slice_in_dim(shard, start, rows, 0)
        return [piece[i : i + PART] for i in range(0, rows, PART)]

    start = jnp.asarray(DOWN_AT, jnp.int32)[dp]
    return jnp.concatenate(
        parts(w_down, start, 96)
        + parts(w_out, dp * 64, 64)
        + parts(w_gate, dp * PART, PART)
        + parts(w_up, dp * PART, PART),
        axis=1,
    )


def late_specs(depth, wide):
    fixed = dict(pipeline_mode=pl.Buffered(1))
    gate = 5 * depth // FTILE
    return [
        pl.BlockSpec((32 * PART, 3 * depth), lambda n: (0, 0), **fixed),
        pl.BlockSpec((32 * PART, depth), lambda n: (0, 3), **fixed),
        pl.BlockSpec((32 * PART, depth), lambda n: (0, 4), **fixed),
        pl.BlockSpec((32 * PART, FTILE), lambda n: (0, gate + n)),
        pl.BlockSpec((32 * PART, FTILE), lambda n: (0, gate + wide // FTILE + n)),
    ]


def place_late(down, first, second, w_out, w_down):
    depth = w_down.shape[1]
    for group in range(32):
        given = slice(group * PART, (group + 1) * PART)
        w_out[group * 64 : group * 64 + PART] = first[given]
        w_out[group * 64 + PART : (group + 1) * 64] = second[given]
        start = group // 4 * 352 + DOWN_AT[group % 4]
        for i in range(3):
            at = start + i * PART
            w_down[at : at + PART] = down[given, i * depth : (i + 1) * depth]


def ffn_forward_kernel(
    gated, more, x, gain, down, out_first, out_second, w_gate, w_up,
    residual, ffn_low, gate_act, up_act, hidden, result, w_out, w_down, total,
):
    step = pl.program_id(0)

    @pl.when(step == 0)
    def _():
        place_late(down, out_first, out_second, w_out, w_down)
        inner = gated.shape[1]
        value = x[...].astype(f32)
        value += jnp.dot(gated[...], w_out[:inner], preferred_element_type=f32)
        value += jnp.dot(more[...], w_out[inner:], preferred_element_type=f32)
        residual[...] = value
        total[...] = value
        scale = lax.rsqrt(jnp.mean(value * value, axis=1, keepdims=True) + norm_eps)
        ffn_low[...] = (value * scale * gain[...]).astype(bf16)

    gate = jnp.dot(ffn_low[...], w_gate[...], preferred_element_type=f32)
    up = jnp.dot(ffn_low[...], w_up[...], preferred_element_type=f32)
    gate_act[...] = gate.astype(bf16)
    up_act[...] = up.astype(bf16)
    low = (gate * jax.nn.sigmoid(gate) * up).astype(bf16)
    hidden[...] = low
    total[...] += jnp.dot(
        low, w_down[pl.ds(pl.multiple_of(step * FTILE, FTILE), FTILE), :],
        preferred_element_type=f32,
    )

    @pl.when(step == pl.num_programs(0) - 1)
    def _():
        result[...] = total[...].astype(bf16)


def ffn_forward(gated, more, x, gain, late):
    rows, depth = x.shape
    wide = (late.shape[1] - 5 * depth) // 2
    tall = gated.shape[1] + more.shape[1]
    still = lambda array: pl.BlockSpec(array.shape, lambda n: (0, 0))
    tile = pl.BlockSpec((rows, FTILE), lambda n: (0, n))
    whole = pl.BlockSpec((rows, depth), lambda n: (0, 0))
    return pl.pallas_call(
        ffn_forward_kernel,
        grid_spec=pltpu.PrefetchScalarGridSpec(
            num_scalar_prefetch=0,
            grid=(wide // FTILE,),
            in_specs=[still(gated), still(more), still(x), still(gain)] + late_specs(depth, wide),
            out_specs=[whole, whole, tile, tile, tile, whole],
            scratch_shapes=[
                pltpu.VMEM((tall, depth), bf16),
                pltpu.VMEM((wide, depth), bf16),
                pltpu.VMEM((rows, depth), f32),
            ],
        ),
        out_shape=[
            jax.ShapeDtypeStruct((rows, depth), f32),
            jax.ShapeDtypeStruct((rows, depth), bf16),
            jax.ShapeDtypeStruct((rows, wide), bf16),
            jax.ShapeDtypeStruct((rows, wide), bf16),
            jax.ShapeDtypeStruct((rows, wide), bf16),
            jax.ShapeDtypeStruct((rows, depth), bf16),
        ],
        name="ffn_forward",
        cost_estimate=cost(27),
    )(gated, more, x, gain, *[late] * 5)


def ffn_backward_kernel(
    cot, residual, gain, gate_act, up_act, down, out_first, out_second, w_gate, w_up,
    gate_low, up_low, grad_residual, mix_low, grad_gated, grad_gain, w_out, w_down, total,
):
    step = pl.program_id(0)

    @pl.when(step == 0)
    def _():
        place_late(down, out_first, out_second, w_out, w_down)
        total[...] = jnp.zeros_like(total)

    grad = lax.dot_general(
        cot[...], w_down[pl.ds(pl.multiple_of(step * FTILE, FTILE), FTILE), :], NT,
        preferred_element_type=f32,
    )
    gate, up = gate_act[...].astype(f32), up_act[...].astype(f32)
    sig = jax.nn.sigmoid(gate)
    low = (grad * up * silu_back(gate, sig)).astype(bf16)
    gate_low[...] = low
    part = lax.dot_general(low, w_gate[...], NT, preferred_element_type=f32)
    low = (grad * (gate * sig)).astype(bf16)
    up_low[...] = low
    total[...] += part + lax.dot_general(low, w_up[...], NT, preferred_element_type=f32)

    @pl.when(step == pl.num_programs(0) - 1)
    def _():
        value, grad = residual[...], total[...]
        scale = lax.rsqrt(jnp.mean(value * value, axis=1, keepdims=True) + norm_eps)
        unit = value * scale
        grad_gain[...] = jnp.sum(grad * unit, axis=0, keepdims=True)
        grad = grad * gain[...]
        grad = scale * (grad - unit * jnp.mean(grad * unit, axis=1, keepdims=True))
        grad = cot[...].astype(f32) + grad
        grad_residual[...] = grad
        low = grad.astype(bf16)
        mix_low[...] = low
        grad_gated[...] = lax.dot_general(low, w_out[...], NT, preferred_element_type=f32)


def ffn_backward(cot, residual, gain, gate_act, up_act, late):
    rows, depth = cot.shape
    wide = gate_act.shape[1]
    tall = 2 * depth
    still = lambda array: pl.BlockSpec(array.shape, lambda n: (0, 0))
    tile = pl.BlockSpec((rows, FTILE), lambda n: (0, n))
    whole = pl.BlockSpec((rows, depth), lambda n: (0, 0))
    return pl.pallas_call(
        ffn_backward_kernel,
        grid_spec=pltpu.PrefetchScalarGridSpec(
            num_scalar_prefetch=0,
            grid=(wide // FTILE,),
            in_specs=[still(cot), still(residual), still(gain), tile, tile] + late_specs(depth, wide),
            out_specs=[
                tile, tile, whole, whole,
                pl.BlockSpec((rows, tall), lambda n: (0, 0)),
                pl.BlockSpec((1, depth), lambda n: (0, 0)),
            ],
            scratch_shapes=[
                pltpu.VMEM((tall, depth), bf16),
                pltpu.VMEM((wide, depth), bf16),
                pltpu.VMEM((rows, depth), f32),
            ],
        ),
        out_shape=[
            jax.ShapeDtypeStruct((rows, wide), bf16),
            jax.ShapeDtypeStruct((rows, wide), bf16),
            jax.ShapeDtypeStruct((rows, depth), f32),
            jax.ShapeDtypeStruct((rows, depth), bf16),
            jax.ShapeDtypeStruct((rows, tall), f32),
            jax.ShapeDtypeStruct((1, depth), f32),
        ],
        name="ffn_backward",
        cost_estimate=cost(35),
    )(cot, residual, gain, gate_act, up_act, *[late] * 5)


def rows_of(array, rows, width):
    count = array.shape[1] // width
    parts = [array[:, i * width : (i + 1) * width] for i in range(count)]
    parts[-1] = parts[-1][: rows - 64 * (count - 1)]
    return jnp.concatenate(parts, axis=0)


def rms_scale(values, gain):
    return values * lax.rsqrt(jnp.mean(values * values, axis=-1, keepdims=True) + norm_eps) * gain


def swiglu(gate_act, up_act):
    return jax.nn.silu(gate_act) * up_act


def exact(left, right, dims=NN):
    return lax.dot_general(left, right, dims, preferred_element_type=f32)


def select_rows(rows, array, dims=NN):
    picks = rows[:, None] == jnp.arange(array.shape[0], dtype=jnp.int32)[None, :]
    return exact(picks.astype(bf16), array, dims).astype(bf16)


def routing(seq_len, dealt_slot, parts, own_index):
    share = MB_TOK // parts
    count = seq_len.shape[0]
    order = jnp.arange(count, dtype=jnp.int32)
    holder = jnp.sum(jnp.where(dealt_slot[None, :] == order[:, None], order[None, :], 0), axis=1)
    piece = seq_len // parts
    begin = jnp.sum(jnp.where(order[None, :] < order[:, None], piece[None, :], 0), axis=1)
    holds = holder[:, None] == order[None, :]
    slot_len = jnp.sum(jnp.where(holds, seq_len[None, :], 0), axis=1)
    slot_len = slot_len.reshape(parts, MICRO, SEQ_MB)
    slot_given = jnp.sum(jnp.where(holds, begin[None, :], 0), axis=1)
    slot_given = slot_given.reshape(parts, MICRO, SEQ_MB)
    slot_piece = slot_len // parts
    slot_row = jnp.arange(share, dtype=jnp.int32)
    place = jnp.arange(MB_TOK, dtype=jnp.int32)
    source = jnp.arange(parts, dtype=jnp.int32)
    micro = jnp.arange(MICRO, dtype=jnp.int32)
    first = jnp.cumsum(slot_piece, axis=2) - slot_piece
    row = slot_row[None, None, :, None]
    inside = (row >= first[:, :, None, :]) & (row < (first + slot_piece)[:, :, None, :])
    send = jnp.sum(
        jnp.where(inside, slot_given[:, :, None, :] + row - first[:, :, None, :], 0), axis=3
    )
    own_len = lax.dynamic_index_in_dim(slot_len, own_index, 0, keepdims=False)
    own_piece = own_len // parts
    own_first = jnp.cumsum(own_piece, axis=1) - own_piece
    own_start = jnp.cumsum(own_len, axis=1) - own_len
    offset = place[None, :, None] - own_start[:, None, :]
    covered = (offset >= 0) & (offset < own_len[:, None, :])
    per = own_piece[:, None, :]
    flat = (
        offset // per * (MICRO * share)
        + micro[:, None, None] * share
        + own_first[:, None, :]
        + offset % per
    )
    arrange = jnp.sum(jnp.where(covered, flat, 0), axis=2).reshape(-1)
    position = jnp.sum(jnp.where(covered, offset, 0), axis=2).reshape(-1)
    label = jnp.sum(
        jnp.where(covered, jnp.arange(SEQ_MB, dtype=jnp.int32)[None, None, :], 0), axis=2
    ).reshape(-1)
    return send.reshape(-1), arrange, position, label


def gate_tables(gate_in, a_log, dt_bias):
    rate = -jnp.exp(a_log) * jax.nn.softplus(gate_in[:, :H] + dt_bias)
    place = jnp.arange(MB_TOK, dtype=jnp.int32)
    lower = (place[:, None] >= place[None, :]).astype(f32)
    total = jnp.einsum(
        "ij,cjh->cih", lower, rate.reshape(MICRO, MB_TOK, H), precision=lax.Precision.HIGHEST
    ).reshape(ROWS, H)
    return total, jax.nn.sigmoid(gate_in[:, H:])


def gather_full(shard):
    reps = lax.axis_size("dp")
    if shard.shape[0] % (8 * reps) == 0:
        rows = shard.shape[0] // reps
        part = lax.dynamic_slice_in_dim(shard, lax.axis_index("dp") * rows, rows, 0)
        return lax.all_gather(part, ("fsdp", "dp"), axis=0, tiled=True)
    return lax.all_gather(shard, "fsdp", axis=0, tiled=True)


def reduce_grad(grad):
    parts, reps = lax.axis_size("fsdp"), lax.axis_size("dp")
    if grad.shape[0] % (8 * parts * reps) == 0:
        part = lax.psum_scatter(grad, ("fsdp", "dp"), scatter_dimension=0, tiled=True)
        return lax.all_gather(part, "dp", axis=0, tiled=True).astype(f32)
    part = lax.psum_scatter(grad, "fsdp", scatter_dimension=0, tiled=True)
    return lax.psum(part, "dp").astype(f32)


def local(
    tokens,
    cotangent,
    lengths,
    dealing,
    gain_mix,
    w_qkv,
    w_gates,
    w_outgate,
    conv_weight,
    a_log,
    dt_bias,
    out_norm_gain,
    w_out,
    gain_ffn,
    w_gate,
    w_up,
    w_down,
):
    parts = lax.axis_size("fsdp")
    own = lax.axis_index("fsdp")
    width = tokens.shape[2]
    share = MB_TOK // parts
    plane = Plane() if (parts, lax.axis_size("dp")) == (8, 4) else None
    send, arrange, position, label = routing(lengths[0], dealing[0], parts, own)

    def exchange(rows):
        return lax.all_to_all(
            rows.reshape(parts, MICRO * share, width),
            "fsdp",
            split_axis=0,
            concat_axis=0,
            tiled=True,
        ).reshape(ROWS, width)

    def give_back(rows):
        return select_rows(send, exchange(select_rows(arrange, rows, TN)), TN)[None]

    def gram(left, right):
        return exact(left, right, TN).astype(bf16)

    small = (gain_mix, gain_ffn, w_gates, conv_weight)
    packed = jnp.concatenate([item.reshape(-1) for item in small])
    if plane:
        packed = plane.gather_small(packed.reshape(-1, 128))
    else:
        packed = lax.all_gather(packed, "fsdp", axis=0, tiled=False)
    packed = packed.reshape(parts, -1)
    full, start = [], 0
    for item in small:
        piece = packed[:, start : start + item.size]
        full.append(piece.reshape((parts * item.shape[0],) + item.shape[1:]))
        start += item.size
    full_gain_mix, full_gain_ffn = full[0].astype(f32), full[1].astype(f32)
    full_gates, taps = full[2], full[3].astype(f32).T

    local_x = select_rows(arrange, exchange(select_rows(send, tokens[0])))

    w_mix = jnp.concatenate([w_qkv, w_outgate], axis=1)
    late = (w_down, w_out, w_gate, w_up)
    if plane:
        units = plane.units()
        late_full = lax.all_gather(late_quarter(*late), ("fsdp", "dp"), axis=0, tiled=True)
        mix_blocks = gather_blocks(plane, plane.half(w_mix))
        widths = (3 * width, 2 * width, w_gate.shape[1], w_up.shape[1])
    else:
        full_mix = gather_full(w_mix)
        full_down, full_out, full_gate, full_up = (gather_full(item) for item in late)

    inputs_f = local_x.astype(f32)
    normed, mix_back = jax.vjp(rms_scale, inputs_f, full_gain_mix)
    normed_low = normed.astype(bf16)
    gate_in = exact(normed_low, full_gates)
    (total, strength), gates_back = jax.vjp(gate_tables, gate_in, a_log, dt_bias)
    spread = lambda item: jnp.broadcast_to(item.astype(f32)[:, None], (ROWS, H))
    table = jnp.stack(
        [total, strength, spread(label), spread(position)] + [jnp.zeros((ROWS, H), f32)] * 4
    )
    col = jnp.transpose(table, (2, 1, 0))
    row = jnp.transpose(table, (2, 0, 1))
    gain = out_norm_gain[None, :]
    if plane:
        projected = project(units, normed_low, mix_blocks, 512)
    else:
        projected = exact(normed_low, full_mix)
    count = H // 2
    firsts = (0, count)
    mixed = [mixer_forward(projected, col, row, taps, gain, firsts[0], count)]
    mixed.append(mixer_forward(projected, col, row, taps, gain, firsts[1], count))
    given_cot = after(cotangent[0], mixed[0][0])
    local_cot = select_rows(arrange, exchange(select_rows(send, given_cot)))
    if plane:
        residual, ffn_low, gate_act, up_act, hidden_low, result = ffn_forward(
            mixed[0][0], mixed[1][0], local_x, full_gain_ffn[None, :], late_full
        )
        down = Reduce(
            plane, gram_blocks(units, hidden_low.T, [local_cot], 1024, widths[0])
        )
        rows_out = select_rows(arrange, after(result, down.send), TN)
        recv_out = exchange(rows_out)
        sent = down.start(rows_out)
        gate_low, up_low, grad_residual, mix_low, grad_gated, grad_gain_ffn = ffn_backward(
            after(local_cot, sent), residual, full_gain_ffn[None, :], gate_act, up_act, late_full
        )
        sent = down.turn(grad_gated)
        gated_t = jnp.concatenate([part[0].T for part in mixed], axis=0)
        wide = widths[1] + widths[2]
        sums = gram_blocks(units, gated_t, [after(mix_low, sent)], 1024, wide)
        sums = gram_blocks(units, ffn_low.T, [gate_low], FTILE, wide, widths[1], sums)
        out_gate_sums = Reduce(plane, sums)
        up = Reduce(
            plane,
            gram_blocks(
                units, ffn_low.T, [after(up_low, out_gate_sums.send)], FTILE, widths[3]
            ),
            split=True,
        )
        sent = down.along(up.send)
        sent = out_gate_sums.start(sent)
    else:
        gated_low = jnp.concatenate([part[0] for part in mixed], axis=1)
        residual = inputs_f + exact(gated_low, full_out)
        ffn_normed, ffn_back = jax.vjp(rms_scale, residual, full_gain_ffn)
        ffn_low = ffn_normed.astype(bf16)
        gate_act = exact(ffn_low, full_gate)
        up_act = exact(ffn_low, full_up)
        hidden, act_back = jax.vjp(swiglu, gate_act, up_act)
        hidden_low = hidden.astype(bf16)
        result = (residual + exact(hidden_low, full_down)).astype(bf16)
        output = give_back(result)
        grad_gate_act, grad_up_act = act_back(exact(local_cot, full_down, NT))
        gate_low, up_low = grad_gate_act.astype(bf16), grad_up_act.astype(bf16)
        grad_part, grad_gain_ffn = ffn_back(
            exact(gate_low, full_gate, NT) + exact(up_low, full_up, NT)
        )
        grad_residual = local_cot.astype(f32) + grad_part
        mix_low = grad_residual.astype(bf16)
        grad_gated = exact(mix_low, full_out, NT)
        late_grads = [
            reduce_grad(gram(left, right))
            for left, right in (
                (hidden_low, local_cot), (gated_low, mix_low), (ffn_low, gate_low),
                (ffn_low, up_low),
            )
        ]
    backs = []
    for part, first in zip(mixed, firsts):
        grad = after(grad_gated, sent) if plane else grad_gated
        backs.append(
            mixer_backward(projected, grad, col, row, taps, gain, part[1], part[2], first)
        )
        if plane and not first:
            sent = up.start(backs[0][0])
            sent = down.across(sent)
    rights = [back[i] for i in range(4) for back in backs]
    dtap_q, dtap_k, dtap_v = (
        jnp.concatenate([back[i] for back in backs], axis=1) for i in (4, 5, 6)
    )
    dgain, dcol, drow = (jnp.concatenate([back[i] for back in backs]) for i in (7, 8, 9))
    if plane:
        left = normed_low.T
        qk = Reduce(plane, gram_blocks(units, left, rights[:4], 512, 2 * H * DK))
        rights[4] = after(rights[4], qk.send)
        vo = Reduce(plane, gram_blocks(units, left, rights[4:], 512, 2 * H * DV), split=True)
        sent = out_gate_sums.turn(vo.send)
        sent = qk.start(sent)
        rights[0] = after(rights[0], sent)
        grad_normed = back_project(units, rights, mix_blocks, width, 512)
        sent = up.beside(grad_normed)
        sent = out_gate_sums.along(sent)
        sent = vo.start(sent)
        sent = down.close(sent)
    else:
        low = jnp.concatenate(rights, axis=1)
        grad_mix = reduce_grad(gram(normed_low, low))
        grad_normed = exact(low, full_mix, NT)
    grad_conv = jnp.concatenate([dtap_q, dtap_k, dtap_v], axis=1).T
    grad_out_gain = jnp.sum(dgain[:, 0], axis=0)
    grad_strength = drow[:, 0].T
    grad_total = dcol[:, :, 0].T - strength * grad_strength
    grad_gate_in, grad_a_log, grad_dt_bias = gates_back((grad_total, grad_strength))
    gate_in_low = grad_gate_in.astype(bf16)
    grad_gates = exact(normed_low, gate_in_low, TN)
    grad_normed = grad_normed + exact(gate_in_low, full_gates, NT)
    grad_part, grad_gain_mix = mix_back(grad_normed)
    grad_inputs = (grad_residual + grad_part).astype(bf16)
    if plane:
        rows_in = select_rows(arrange, after(grad_inputs, sent), TN)
        recv_in = exchange(rows_in)
        sent = qk.turn(rows_in)
        sent = up.turn(sent)
        sent = out_gate_sums.across(sent)
        output = select_rows(send, after(recv_out, sent), TN)[None]
    else:
        input_grad = give_back(grad_inputs)

    small_grads = (grad_gain_mix, grad_gain_ffn, grad_gates, grad_conv)
    alone = (grad_a_log, grad_dt_bias, grad_out_gain)
    sums = jnp.concatenate(
        [item.reshape(parts, -1) for item in small_grads]
        + [jnp.broadcast_to(jnp.concatenate(alone)[None], (parts, 2 * H + DV))],
        axis=1,
    )
    if plane:
        sums = plane.sum_small(after(sums, sent))
        sent = qk.along(sums)
        sent = vo.beside(sent)
        sent = up.along(sent)
        sent = out_gate_sums.close(sent)
        input_grad = select_rows(send, after(recv_in, sent), TN)[None]
        sent = qk.across(input_grad)
        sent = vo.turn(sent)
        sent = up.across(sent)
        sent = qk.close(sent)
        sent = vo.along(sent)
        sent = up.close(sent)
        sent = vo.across(sent)
        vo.close(sent)
        out_gate_halves = out_gate_sums.halves()
        cut = widths[1]

        def whole(halves, rows, columns):
            return jnp.concatenate(
                [rows_of(part, rows // 2, columns) for part in halves], axis=0
            ).astype(f32)

        late_grads = (
            whole(down.halves(), w_down.shape[0], width),
            whole([part[:, :cut] for part in out_gate_halves], w_out.shape[0], width),
            jnp.concatenate([part[:, cut:] for part in out_gate_halves], axis=0).astype(f32),
            jnp.concatenate(up.halves(), axis=0).astype(f32),
        )
        qk_grad, vo_grad = (
            jnp.concatenate(item.halves(), axis=0).astype(f32) for item in (qk, vo)
        )
        grad_qkv = jnp.concatenate([qk_grad, vo_grad[:, : H * DV]], axis=1)
        grad_outgate = vo_grad[:, H * DV :]
    else:
        sums = lax.psum(sums, ("fsdp", "dp"))
        grad_qkv, grad_outgate = grad_mix[:, : w_qkv.shape[1]], grad_mix[:, w_qkv.shape[1] :]
    sums = lax.dynamic_index_in_dim(sums, own, 0, keepdims=False)
    ready, start = [], 0
    for item in (gain_mix, gain_ffn, w_gates, conv_weight) + alone:
        ready.append(sums[start : start + item.size].reshape(item.shape))
        start += item.size
    return (
        output,
        input_grad,
        ready[0],
        grad_qkv,
        ready[2],
        grad_outgate,
        ready[3],
        ready[4],
        ready[5],
        ready[6],
        late_grads[1],
        ready[1],
        late_grads[2],
        late_grads[3],
        late_grads[0],
    )


def solution(mesh):
    in_specs = (
        P("dp", "fsdp", None),
        P("dp", "fsdp", None),
        P("dp", None),
        P("dp", None),
        P("fsdp"),
        P("fsdp", None),
        P("fsdp", None),
        P("fsdp", None),
        P("fsdp", None),
        P(),
        P(),
        P(),
        P("fsdp", None),
        P("fsdp"),
        P("fsdp", None),
        P("fsdp", None),
        P("fsdp", None),
    )
    out_specs = (
        P("dp", "fsdp", None),
        P("dp", "fsdp", None),
        P("fsdp"),
        P("fsdp", None),
        P("fsdp", None),
        P("fsdp", None),
        P("fsdp", None),
        P(),
        P(),
        P(),
        P("fsdp", None),
        P("fsdp"),
        P("fsdp", None),
        P("fsdp", None),
        P("fsdp", None),
    )
    return jax.shard_map(local, mesh=mesh, in_specs=in_specs, out_specs=out_specs, check_vma=False)
```

```python
from functools import partial

import jax
import jax.numpy as jnp
from jax import lax
from jax.experimental import pallas as pl
from jax.experimental.pallas import tpu as pltpu
from jax.sharding import PartitionSpec as P

H = 8
DK = 128
DV = 256
TAPS = 4
MB_TOK = 256
MICRO = 2
SEQ_MB = 2
ROWS = MB_TOK * MICRO

norm_eps = 1e-05
unit_eps = 1e-06
f32 = jnp.float32
bf16 = jnp.bfloat16
NN = (((1,), (0,)), ((), ()))
NT = (((1,), (1,)), ((), ()))
TN = (((0,), (0,)), ((), ()))


def mm(left, right, dims=NN):
    return lax.dot_general(
        left.astype(bf16), right.astype(bf16), dims, preferred_element_type=f32
    )


def halves(value):
    high = value.astype(bf16)
    return high, (value - high.astype(f32)).astype(bf16)


def mm_split(left, right, dims=NN):
    return mm(left[0], right[0], dims) + (mm(left[0], right[1], dims) + mm(left[1], right[0], dims))


def conv_taps(signal, weight, position):
    total = signal * weight[TAPS - 1 : TAPS]
    shifted = []
    for delay in range(1, TAPS):
        moved = jnp.where(position >= delay, pltpu.roll(signal, delay, 0), 0.0)
        shifted.append(moved)
        total = total + moved * weight[TAPS - 1 - delay : TAPS - delay]
    return total, shifted


def unit_rows(value):
    return lax.rsqrt(jnp.sum(value * value, axis=1, keepdims=True) + unit_eps)


def chain_masks(label_col, label_row):
    size = MB_TOK
    row = lax.broadcasted_iota(jnp.int32, (size, size), 0)
    col = lax.broadcasted_iota(jnp.int32, (size, size), 1)
    same = label_col == label_row
    return row, col, (row >= col) & same, (row > col) & same


def unit_lower_inverses(systems):
    row = lax.broadcasted_iota(jnp.int32, (MB_TOK, MB_TOK), 0)
    col = lax.broadcasted_iota(jnp.int32, (MB_TOK, MB_TOK), 1)
    apart = row ^ col
    eye = jnp.where(row == col, 1.0, 0.0)
    inverses = [eye - jnp.where(apart == 1, system, 0.0) for system in systems]
    lows = [system.astype(bf16) for system in systems]
    level = 1
    while (1 << level) < MB_TOK:
        now = (apart >> level) == 1
        pairs = [inverse.astype(bf16) for inverse in inverses]
        halfway = [mm(pair, jnp.where(now, low, 0)) for pair, low in zip(pairs, lows)]
        inverses = [
            inverse - mm(half, pair) for inverse, half, pair in zip(inverses, halfway, pairs)
        ]
        level += 1
    pairs = [halves(inverse) for inverse in inverses]
    rests = [
        eye - inverse - mm_split(halves(system), pair)
        for inverse, system, pair in zip(inverses, systems, pairs)
    ]
    return [inverse + mm(pair[0], rest) for inverse, pair, rest in zip(inverses, pairs, rests)]


def mixer_forward_kernel(
    pq, pk, pv, og, col, row, wq, wk, wv, gain, gated_ref, turned_ref, inverse_ref, pseudo_ref
):
    position = col[0, :, 3:4]
    query, key, value = (
        pre * jax.nn.sigmoid(pre)
        for pre in (
            conv_taps(pq[...], wq[...], position)[0],
            conv_taps(pk[...], wk[...], position)[0],
            conv_taps(pv[...], wv[...], position)[0],
        )
    )
    query = (query * (unit_rows(query) * DK ** (-0.5))).astype(bf16)
    key = (key * unit_rows(key)).astype(bf16)
    chains = [slice(chain * MB_TOK, (chain + 1) * MB_TOK) for chain in range(MICRO)]
    systems, attends = [], []
    for rows in chains:
        _, _, lower, strict = chain_masks(col[0, rows, 2:3], row[0, 2:3, rows])
        spread = jnp.where(lower, col[0, rows, 0:1] - row[0, 0:1, rows], 0.0)
        weight = jnp.exp(spread) * row[0, 1:2, rows]
        systems.append(jnp.where(strict, weight * mm(key[rows], key[rows], NT), 0.0))
        attends.append(jnp.where(lower, weight * mm(query[rows], key[rows], NT), 0.0).astype(bf16))
    inverses = unit_lower_inverses(systems)
    for rows, inverse, attend in zip(chains, inverses, attends):
        low = inverse.astype(bf16)
        inverse_ref[0, rows] = low
        pseudo = mm(low, value[rows]).astype(bf16)
        pseudo_ref[0, rows] = pseudo
        heads_out = mm(attend, pseudo)
        scale = lax.rsqrt(jnp.mean(heads_out * heads_out, axis=1, keepdims=True) + norm_eps)
        gate = og[rows]
        gated = heads_out * scale * gain[...] * (gate * jax.nn.sigmoid(gate))
        gated_ref[rows] = gated.astype(bf16)
        turned_ref[:, rows] = gated.T.astype(bf16)


def silu_back(pre, sig):
    return sig * (1.0 + pre * (1.0 - sig))


def conv_back(grad, shifted, signal, weight, position):
    out = grad * weight[TAPS - 1 : TAPS]
    taps = [jnp.sum(grad * signal, axis=0, keepdims=True)]
    for delay in range(1, TAPS):
        taps.append(jnp.sum(grad * shifted[delay - 1], axis=0, keepdims=True))
        kept = jnp.where(position >= delay, grad, 0.0)
        out = out + pltpu.roll(kept, ROWS - delay, 0) * weight[TAPS - 1 - delay : TAPS - delay]
    return out, jnp.concatenate(taps[::-1], axis=0)


def mixer_backward_kernel(
    pq, pk, pv, og, gg, col, row, wq, wk, wv, gain, inverse_ref, pseudo_ref,
    dq_ref, dk_ref, dv_ref, dog_ref, dwq_ref, dwk_ref, dwv_ref, dgain_ref, dcol_ref, drow_ref,
    gq_s, gk_s, gv_s,
):
    position = col[0, :, 3:4]
    pres = []
    for signal, weight in ((pq, wq), (pk, wk), (pv, wv)):
        pre, shifted = conv_taps(signal[...], weight[...], position)
        pres.append((pre, jax.nn.sigmoid(pre), shifted))
    mixed_q, mixed_k, value = (pre * sig for pre, sig, _ in pres)
    unit_q, unit_k = unit_rows(mixed_q), unit_rows(mixed_k)
    query = mixed_q * (unit_q * DK ** (-0.5))
    key = mixed_k * unit_k
    gain_total = jnp.zeros((1, DV), f32)
    for chain in range(MICRO):
        rows = slice(chain * MB_TOK, (chain + 1) * MB_TOK)
        at, to, lower, strict = chain_masks(col[0, rows, 2:3], row[0, 2:3, rows])
        spread = jnp.where(lower, col[0, rows, 0:1] - row[0, 0:1, rows], 0.0)
        fade = jnp.where(lower, jnp.exp(spread), 0.0)
        beta = row[0, 1:2, rows]
        q, k = query[rows].astype(bf16), key[rows].astype(bf16)
        system = jnp.where(strict, fade, 0.0) * mm(k, k, NT)
        attend = fade * mm(q, k, NT)
        spread_attend = (attend * beta).astype(bf16)
        pseudo_low = pseudo_ref[0, rows]
        heads_out = mm(spread_attend, pseudo_low)
        scale = lax.rsqrt(jnp.mean(heads_out * heads_out, axis=1, keepdims=True) + norm_eps)
        gate = og[rows]
        sig = jax.nn.sigmoid(gate)
        grad = gg[rows]
        unit = heads_out * scale
        dog_ref[rows] = (grad * unit * gain[...] * silu_back(gate, sig)).astype(bf16)
        grad = grad * (gate * sig)
        gain_total = gain_total + jnp.sum(grad * unit, axis=0, keepdims=True)
        grad = grad * gain[...]
        grad_out = scale * (grad - unit * jnp.mean(grad * unit, axis=1, keepdims=True))
        out_low = grad_out.astype(bf16)
        grad_attend = mm(out_low, pseudo_low, NT)
        grad_value = mm(inverse_ref[0, rows], mm(spread_attend, out_low, TN), TN)
        grad_system = -mm(grad_value, pseudo_low, NT)
        both = grad_attend * attend + grad_system * system
        drow_ref[0, 0:1, rows] = jnp.sum(both, axis=0, keepdims=True)
        dcol_ref[0, rows] = jnp.broadcast_to(
            jnp.sum(both * beta, axis=1, keepdims=True), (MB_TOK, 8)
        )
        weight = fade * beta
        from_attend = (grad_attend * weight).astype(bf16)
        from_system = (jnp.where(strict, grad_system, 0.0) * weight).astype(bf16)
        gq_s[rows] = mm(from_attend, k)
        gk_s[rows] = mm(from_attend, q, TN) + (mm(from_system, k) + mm(from_system, k, TN))
        gv_s[rows] = grad_value
    drow_ref[0, 1:8] = jnp.zeros((7, ROWS), f32)
    dgain_ref[0] = jnp.broadcast_to(gain_total, (8, DV))
    grad_q = gq_s[...] * DK ** (-0.5)
    unit = mixed_q * unit_q
    grad_q = unit_q * (grad_q - unit * jnp.sum(grad_q * unit, axis=1, keepdims=True))
    grad_k = gk_s[...]
    grad_k = unit_k * (grad_k - key * jnp.sum(grad_k * key, axis=1, keepdims=True))
    for grad, (pre, sig, shifted), signal, weight, out, dw in (
        (grad_q, pres[0], pq, wq, dq_ref, dwq_ref),
        (grad_k, pres[1], pk, wk, dk_ref, dwk_ref),
        (gv_s[...], pres[2], pv, wv, dv_ref, dwv_ref),
    ):
        back, taps = conv_back(
            grad * silu_back(pre, sig), shifted, signal[...], weight[...], position
        )
        out[...] = back.astype(bf16)
        dw[...] = taps


def columns(width, start):
    return pl.BlockSpec((ROWS, width), lambda head: (0, head + start))


def tap_columns(width, start):
    return pl.BlockSpec((TAPS, width), lambda head: (0, head + start))


def per_head(*shape, start=0):
    return pl.BlockSpec((1,) + shape, lambda head: (head + start,) + (0,) * len(shape))


def mixer_inputs(first):
    return (
        [columns(DK, first), columns(DK, H + first), columns(DV, H + first)]
        + [columns(DV, 2 * H + first)],
        [per_head(ROWS, 8, start=first), per_head(8, ROWS, start=first)]
        + [tap_columns(DK, first), tap_columns(DK, H + first), tap_columns(DV, H + first)]
        + [pl.BlockSpec((1, DV), lambda head: (0, 0))],
    )


def mixer_forward(projected, col, row, taps, gain, first, count):
    start, rest = mixer_inputs(first)
    return pl.pallas_call(
        mixer_forward_kernel,
        grid=(count,),
        in_specs=start + rest,
        out_specs=[
            columns(DV, 0),
            pl.BlockSpec((DV, ROWS), lambda head: (head, 0)),
            per_head(ROWS, MB_TOK),
            per_head(ROWS, DV),
        ],
        out_shape=[
            jax.ShapeDtypeStruct((ROWS, count * DV), bf16),
            jax.ShapeDtypeStruct((count * DV, ROWS), bf16),
            jax.ShapeDtypeStruct((count, ROWS, MB_TOK), bf16),
            jax.ShapeDtypeStruct((count, ROWS, DV), bf16),
        ],
        name="mixer_forward",
        cost_estimate=cost(4.4 * count),
    )(projected, projected, projected, projected, col, row, taps, taps, taps, gain)


def mixer_backward(projected, grad_gated, col, row, taps, gain, inverse, pseudo, first):
    start, rest = mixer_inputs(first)
    count = inverse.shape[0]
    return pl.pallas_call(
        mixer_backward_kernel,
        grid=(count,),
        in_specs=start
        + [columns(DV, first)]
        + rest
        + [per_head(ROWS, MB_TOK), per_head(ROWS, DV)],
        out_specs=[columns(DK, 0), columns(DK, 0), columns(DV, 0), columns(DV, 0)]
        + [tap_columns(DK, 0), tap_columns(DK, 0), tap_columns(DV, 0)]
        + [per_head(8, DV), per_head(ROWS, 8), per_head(8, ROWS)],
        out_shape=[
            jax.ShapeDtypeStruct((ROWS, count * DK), bf16),
            jax.ShapeDtypeStruct((ROWS, count * DK), bf16),
            jax.ShapeDtypeStruct((ROWS, count * DV), bf16),
            jax.ShapeDtypeStruct((ROWS, count * DV), bf16),
            jax.ShapeDtypeStruct((TAPS, count * DK), f32),
            jax.ShapeDtypeStruct((TAPS, count * DK), f32),
            jax.ShapeDtypeStruct((TAPS, count * DV), f32),
            jax.ShapeDtypeStruct((count, 8, DV), f32),
            jax.ShapeDtypeStruct((count, ROWS, 8), f32),
            jax.ShapeDtypeStruct((count, 8, ROWS), f32),
        ],
        scratch_shapes=[
            pltpu.VMEM((ROWS, DK), f32),
            pltpu.VMEM((ROWS, DK), f32),
            pltpu.VMEM((ROWS, DV), f32),
        ],
        name="mixer_backward",
        cost_estimate=cost(4.6 * count),
    )(
        projected, projected, projected, projected, grad_gated, col, row,
        taps, taps, taps, gain, inverse, pseudo,
    )


BLOCKS = tuple((dz, dx) for dx in (1, 0) for dz in (1, 3, 0, 2))


class Plane:
    def __init__(self):
        fsdp, dp = lax.axis_index("fsdp"), lax.axis_index("dp")
        self.z, self.x = fsdp // 2, fsdp % 2
        self.y, self.core = dp // 2, dp % 2

    @staticmethod
    def move(value, dz=0, dx=0, dy=0, dc=0):
        flip = (dz * 2 + dx) * 4 + dy * 2 + dc
        return lax.ppermute(value, ("fsdp", "dp"), [(here, here ^ flip) for here in range(32)])

    def units(self):
        dz, dx = (jnp.asarray([at[i] for at in BLOCKS], jnp.int32) for i in (0, 1))
        base = ((self.z ^ dz) * 2 + (self.x ^ dx)) * 2
        return jnp.concatenate([base + self.core, base + 1 - self.core])

    def mine(self, half):
        rows = half.shape[0] // 2
        return lax.dynamic_slice_in_dim(half, self.y * rows, rows, 0)

    def join(self, mine, other):
        first = self.y == 0
        return jnp.concatenate(
            [jnp.where(first, mine, other), jnp.where(first, other, mine)], axis=0
        )

    def half(self, shard):
        rows = shard.shape[0] // 2
        return lax.dynamic_slice_in_dim(shard, self.core * rows, rows, 0)

def after(value, *others):
    return lax.optimization_barrier((value,) + others)[0]


def summed(*terms):
    return sum(term.astype(f32) for term in terms).astype(bf16)


class Gather:
    def __init__(self, plane, held):
        self.plane = plane
        self.got = {(0, 0): held}
        self.from_core = {}

    def pass_to(self, new, old, **step):
        self.got[new] = self.plane.move(self.got[old], **step)

    def share(self, *blocks):
        for at in blocks:
            self.from_core[at] = self.plane.move(self.got[at], dc=1)

    def wait(self, blocks, *others):
        for at in blocks:
            self.got[at] = after(self.got[at], *others)


class Reduce:
    def __init__(self, plane, sums, split=False):
        self.plane, self.split = plane, split
        self.keep, self.send = sums
        self.back = plane.move(self.send, dc=1)

    def start(self, *others):
        back = after(self.back, *others)
        if not self.split:
            self.part = summed(self.keep[4:], back[4:])
            return self._beside(summed(self.keep[:4], back[:4]))

        def take(array, at):
            return lax.dynamic_slice_in_dim(array, at * 32, 32, 1)

        y = self.plane.y
        self.mine = summed(take(self.keep, y), take(back, y))
        sent = summed(take(self.keep, 1 - y), take(back, 1 - y))
        self.from_y = self.plane.move(sent, dy=1)
        return sent

    def _beside(self, sent):
        self.from_x = self.plane.move(sent, dx=1)
        return sent

    def beside(self, *others):
        from_y = after(self.from_y, *others)
        self.part = summed(self.mine[4:], from_y[4:])
        return self._beside(summed(self.mine[:4], from_y[:4]))

    def turn(self, *others):
        from_x = after(self.from_x, *others)
        sent = summed(self.part[:2], from_x[:2])
        self.rest = summed(self.part[2:], from_x[2:])
        self.from_z = self.plane.move(sent, dz=1)
        return sent

    def along(self, *others):
        self.near = after(self.from_z, *others)
        sent = summed(self.rest[1], self.near[1])
        self.far = self.plane.move(sent, dz=2)
        return sent

    def across(self, *others):
        self.total = summed(self.rest[0], self.near[0], after(self.far, *others))
        self.other = self.plane.move(self.total, dy=1)
        return self.total

    def close(self, *others):
        other = after(self.other, *others)
        if self.split:
            first = self.plane.y == 0
            total = jnp.concatenate(
                [jnp.where(first, self.total, other), jnp.where(first, other, self.total)], axis=0
            )
        else:
            total = summed(self.total, other)
        self.total, self.other = total, self.plane.move(total, dc=1)
        return total

    def halves(self):
        first = self.plane.core == 0
        return (
            jnp.where(first, self.total, self.other),
            jnp.where(first, self.other, self.total),
        )


def cost(us):
    return pl.CostEstimate(
        flops=int(us * 1.0e7), transcendentals=0, bytes_accessed=int(us * 3.0e4)
    )


def place(weight, units, blocks, rows, parts=1):
    width = weight.shape[1]
    for i, block in enumerate(blocks):
        for part in range(parts):
            count = min(rows - 64 * part, 64)
            start = pl.multiple_of(units[i] * rows + 64 * part, 16)
            weight[pl.ds(start, count), :] = block[:count, part * width : (part + 1) * width]


def project_kernel(units, x_ref, *refs):
    blocks, y_ref, weight = refs[:16], refs[16], refs[17]
    place(weight, units, blocks, 64)
    y_ref[...] = jnp.dot(x_ref[...], weight[...], preferred_element_type=f32)


def project(units, value, blocks, tile):
    width = blocks[0].shape[1]
    rows, depth = value.shape
    return pl.pallas_call(
        project_kernel,
        grid_spec=pltpu.PrefetchScalarGridSpec(
            num_scalar_prefetch=1,
            grid=(width // tile,),
            in_specs=[pl.BlockSpec((rows, depth), lambda n, s: (0, 0))]
            + [pl.BlockSpec((64, tile), lambda n, s: (0, n))] * 16,
            out_specs=pl.BlockSpec((rows, tile), lambda n, s: (0, n)),
            scratch_shapes=[pltpu.VMEM((depth, tile), bf16)],
        ),
        out_shape=jax.ShapeDtypeStruct((rows, width), f32),
        name="project",
        cost_estimate=cost(17),
    )(units, value, *blocks)


def tiles_of(arrays, tile):
    specs, firsts, first = [], [], 0
    for array in arrays:
        count = array.shape[1] // tile

        def index(n, s, first=first, count=count):
            return (0, jnp.clip(n - first, 0, count - 1))

        specs.append(pl.BlockSpec((array.shape[0], tile), index))
        firsts.append(first)
        first += count
    return specs, firsts, first


def pick(step, firsts, refs, chosen):
    for i, ref in enumerate(refs):
        here = step >= firsts[i]
        if i + 1 < len(refs):
            here = here & (step < firsts[i + 1])

        @pl.when(here)
        def _():
            chosen[...] = ref[...]


def back_project_kernel(firsts, units, *refs):
    rights, blocks = refs[: len(firsts)], refs[len(firsts) : len(firsts) + 16]
    out_ref, chosen, weight = refs[len(firsts) + 16 :]
    step = pl.program_id(0)
    pick(step, firsts, rights, chosen)
    place(weight, units, blocks, 64)
    part = lax.dot_general(chosen[...], weight[...], NT, preferred_element_type=f32)

    @pl.when(step == 0)
    def _():
        out_ref[...] = part

    @pl.when(step > 0)
    def _():
        out_ref[...] += part


def back_project(units, rights, blocks, depth, tile):
    specs, firsts, steps = tiles_of(rights, tile)
    rows = rights[0].shape[0]
    return pl.pallas_call(
        partial(back_project_kernel, tuple(firsts)),
        grid_spec=pltpu.PrefetchScalarGridSpec(
            num_scalar_prefetch=1,
            grid=(steps,),
            in_specs=specs + [pl.BlockSpec((64, tile), lambda n, s: (0, n))] * 16,
            out_specs=pl.BlockSpec((rows, depth), lambda n, s: (0, 0)),
            scratch_shapes=[pltpu.VMEM((rows, tile), bf16), pltpu.VMEM((depth, tile), bf16)],
        ),
        out_shape=jax.ShapeDtypeStruct((rows, depth), f32),
        name="back_project",
        cost_estimate=cost(18),
    )(units, *rights, *blocks)


def gram_kernel(firsts, rows, units, left_ref, *refs):
    rights = refs[: len(firsts)]
    keep, send, chosen, total = refs[-4:]
    step, part = pl.program_id(0), pl.program_id(1)

    @pl.when(part == 0)
    def _():
        pick(step, firsts, rights, chosen)
        total[0 : left_ref.shape[0], :] = jnp.dot(
            left_ref[...], chosen[...], preferred_element_type=f32
        )

    def block(i):
        value = total[pl.ds(pl.multiple_of(units[i] * rows + part * 64, 16), 64), :]
        if rows % 64:
            inside = lax.broadcasted_iota(jnp.int32, value.shape, 0) < rows - part * 64
            value = jnp.where(inside, value, 0.0)
        return value.astype(bf16)

    for i in range(8):
        keep[i] = block(i)
        send[i] = block(8 + i)


def gram_blocks(units, left, rights, tile, width, base=0, into=()):
    depth, inner = left.shape
    rows = depth // 16
    parts = -(-rows // 64)
    specs, firsts, steps = tiles_of(rights, tile)
    specs = [
        pl.BlockSpec(spec.block_shape, lambda n, p, s, index=spec.index_map: index(n, s))
        for spec in specs
    ]
    first = base // tile

    def column(n, p, s):
        return (0, first + p * steps + n)

    whole = pl.BlockSpec(memory_space=pl.ANY)
    out = pl.pallas_call(
        partial(gram_kernel, tuple(firsts), rows),
        grid_spec=pltpu.PrefetchScalarGridSpec(
            num_scalar_prefetch=1,
            grid=(steps, parts),
            in_specs=[pl.BlockSpec((depth, inner), lambda n, p, s: (0, 0))]
            + specs
            + [whole] * len(into),
            out_specs=[pl.BlockSpec((8, 64, tile), lambda n, p, s: (0,) + column(n, p, s))] * 2,
            scratch_shapes=[
                pltpu.VMEM((inner, tile), bf16),
                pltpu.VMEM((depth + 64, tile), f32),
            ],
        ),
        out_shape=[jax.ShapeDtypeStruct((8, 64, width), bf16)] * 2,
        input_output_aliases={2 + len(rights) + i: i for i in range(len(into))},
        name="gram_blocks",
        cost_estimate=cost(steps * tile * depth / 2.9e5),
    )(units, left, *rights, *into)
    return list(out)


FTILE = 256


PART = 32
DOWN_AT = (0, 96, 176, 256)


def late_quarter(w_down, w_out, w_gate, w_up):
    dp = lax.axis_index("dp")

    def parts(shard, start, rows):
        piece = lax.dynamic_slice_in_dim(shard, start, rows, 0)
        return [piece[i : i + PART] for i in range(0, rows, PART)]

    start = jnp.asarray(DOWN_AT, jnp.int32)[dp]
    return jnp.concatenate(
        parts(w_down, start, 96)
        + parts(w_out, dp * 64, 64)
        + parts(w_gate, dp * PART, PART)
        + parts(w_up, dp * PART, PART),
        axis=1,
    )


def late_specs(depth, wide):
    fixed = dict(pipeline_mode=pl.Buffered(1))
    gate = 5 * depth // FTILE
    up = gate + wide // FTILE
    return [
        pl.BlockSpec((32 * PART, 3 * depth), lambda n: (0, 0), **fixed),
        pl.BlockSpec((32 * PART, depth), lambda n: (0, 3), **fixed),
        pl.BlockSpec((32 * PART, depth), lambda n: (0, 4), **fixed),
        pl.BlockSpec((32 * PART, FTILE), lambda n: (0, gate + n)),
        pl.BlockSpec((32 * PART, FTILE), lambda n: (0, up + n)),
    ]


def place_late(down, first, second, w_out, w_down):
    depth = w_down.shape[1]
    for group in range(32):
        given = slice(group * PART, (group + 1) * PART)
        w_out[group * 64 : group * 64 + PART] = first[given]
        w_out[group * 64 + PART : (group + 1) * 64] = second[given]
        start = group // 4 * 352 + DOWN_AT[group % 4]
        for i in range(3):
            at = start + i * PART
            w_down[at : at + PART] = down[given, i * depth : (i + 1) * depth]


def ffn_forward_kernel(
    gated, more, x, gain, down, out_first, out_second, w_gate, w_up,
    residual, ffn_turned, gate_act, up_act, hidden_turned, result, w_out, w_down, total, ffn_low,
):
    step = pl.program_id(0)

    @pl.when(step == 0)
    def _():
        place_late(down, out_first, out_second, w_out, w_down)
        inner = gated.shape[1]
        value = x[...].astype(f32)
        value += jnp.dot(gated[...], w_out[:inner], preferred_element_type=f32)
        value += jnp.dot(more[...], w_out[inner:], preferred_element_type=f32)
        residual[...] = value
        total[...] = value
        scale = lax.rsqrt(jnp.mean(value * value, axis=1, keepdims=True) + norm_eps)
        normed = value * scale * gain[...]
        ffn_low[...] = normed.astype(bf16)
        ffn_turned[...] = normed.T.astype(bf16)

    gate = jnp.dot(ffn_low[...], w_gate[...], preferred_element_type=f32)
    up = jnp.dot(ffn_low[...], w_up[...], preferred_element_type=f32)
    gate_act[...] = gate.astype(bf16)
    up_act[...] = up.astype(bf16)
    hidden = gate * jax.nn.sigmoid(gate) * up
    hidden_turned[...] = hidden.T.astype(bf16)
    low = hidden.astype(bf16)
    total[...] += jnp.dot(
        low, w_down[pl.ds(pl.multiple_of(step * FTILE, FTILE), FTILE), :],
        preferred_element_type=f32,
    )

    @pl.when(step == pl.num_programs(0) - 1)
    def _():
        result[...] = total[...].astype(bf16)


def ffn_forward(gated, more, x, gain, late):
    rows, depth = x.shape
    wide = (late.shape[1] - 5 * depth) // 2
    tall = gated.shape[1] + more.shape[1]
    still = lambda array: pl.BlockSpec(array.shape, lambda n: (0, 0))
    tile = pl.BlockSpec((rows, FTILE), lambda n: (0, n))
    whole = pl.BlockSpec((rows, depth), lambda n: (0, 0))
    return pl.pallas_call(
        ffn_forward_kernel,
        grid_spec=pltpu.PrefetchScalarGridSpec(
            num_scalar_prefetch=0,
            grid=(wide // FTILE,),
            in_specs=[still(gated), still(more), still(x), still(gain)] + late_specs(depth, wide),
            out_specs=[
                whole,
                pl.BlockSpec((depth, rows), lambda n: (0, 0)),
                tile,
                tile,
                pl.BlockSpec((FTILE, rows), lambda n: (n, 0)),
                whole,
            ],
            scratch_shapes=[
                pltpu.VMEM((tall, depth), bf16),
                pltpu.VMEM((wide, depth), bf16),
                pltpu.VMEM((rows, depth), f32),
                pltpu.VMEM((rows, depth), bf16),
            ],
        ),
        out_shape=[
            jax.ShapeDtypeStruct((rows, depth), f32),
            jax.ShapeDtypeStruct((depth, rows), bf16),
            jax.ShapeDtypeStruct((rows, wide), bf16),
            jax.ShapeDtypeStruct((rows, wide), bf16),
            jax.ShapeDtypeStruct((wide, rows), bf16),
            jax.ShapeDtypeStruct((rows, depth), bf16),
        ],
        name="ffn_forward",
        cost_estimate=cost(27),
    )(gated, more, x, gain, *[late] * 5)


def ffn_backward_kernel(
    cot, residual, gain, gate_act, up_act, down, out_first, out_second, w_gate, w_up,
    gate_low, up_low, grad_residual, mix_low, grad_gated, grad_gain, w_out, w_down, total,
):
    step = pl.program_id(0)

    @pl.when(step == 0)
    def _():
        place_late(down, out_first, out_second, w_out, w_down)
        total[...] = jnp.zeros_like(total)

    grad = lax.dot_general(
        cot[...], w_down[pl.ds(pl.multiple_of(step * FTILE, FTILE), FTILE), :], NT,
        preferred_element_type=f32,
    )
    gate, up = gate_act[...].astype(f32), up_act[...].astype(f32)
    sig = jax.nn.sigmoid(gate)
    low = (grad * up * silu_back(gate, sig)).astype(bf16)
    gate_low[...] = low
    part = lax.dot_general(low, w_gate[...], NT, preferred_element_type=f32)
    low = (grad * (gate * sig)).astype(bf16)
    up_low[...] = low
    total[...] += part + lax.dot_general(low, w_up[...], NT, preferred_element_type=f32)

    @pl.when(step == pl.num_programs(0) - 1)
    def _():
        value, grad = residual[...], total[...]
        scale = lax.rsqrt(jnp.mean(value * value, axis=1, keepdims=True) + norm_eps)
        unit = value * scale
        grad_gain[...] = jnp.sum(grad * unit, axis=0, keepdims=True)
        grad = grad * gain[...]
        grad = scale * (grad - unit * jnp.mean(grad * unit, axis=1, keepdims=True))
        grad = cot[...].astype(f32) + grad
        grad_residual[...] = grad
        low = grad.astype(bf16)
        mix_low[...] = low
        grad_gated[...] = lax.dot_general(low, w_out[...], NT, preferred_element_type=f32)


def ffn_backward(cot, residual, gain, gate_act, up_act, late):
    rows, depth = cot.shape
    wide = gate_act.shape[1]
    tall = 2 * depth
    still = lambda array: pl.BlockSpec(array.shape, lambda n: (0, 0))
    tile = pl.BlockSpec((rows, FTILE), lambda n: (0, n))
    whole = pl.BlockSpec((rows, depth), lambda n: (0, 0))
    return pl.pallas_call(
        ffn_backward_kernel,
        grid_spec=pltpu.PrefetchScalarGridSpec(
            num_scalar_prefetch=0,
            grid=(wide // FTILE,),
            in_specs=[still(cot), still(residual), still(gain), tile, tile] + late_specs(depth, wide),
            out_specs=[
                tile, tile, whole, whole,
                pl.BlockSpec((rows, tall), lambda n: (0, 0)),
                pl.BlockSpec((1, depth), lambda n: (0, 0)),
            ],
            scratch_shapes=[
                pltpu.VMEM((tall, depth), bf16),
                pltpu.VMEM((wide, depth), bf16),
                pltpu.VMEM((rows, depth), f32),
            ],
        ),
        out_shape=[
            jax.ShapeDtypeStruct((rows, wide), bf16),
            jax.ShapeDtypeStruct((rows, wide), bf16),
            jax.ShapeDtypeStruct((rows, depth), f32),
            jax.ShapeDtypeStruct((rows, depth), bf16),
            jax.ShapeDtypeStruct((rows, tall), f32),
            jax.ShapeDtypeStruct((1, depth), f32),
        ],
        name="ffn_backward",
        cost_estimate=cost(35),
    )(cot, residual, gain, gate_act, up_act, *[late] * 5)


def rows_of(array, rows, width):
    count = array.shape[1] // width
    parts = [array[:, i * width : (i + 1) * width] for i in range(count)]
    parts[-1] = parts[-1][: rows - 64 * (count - 1)]
    return jnp.concatenate(parts, axis=0)


def rms_scale(values, gain):
    return values * lax.rsqrt(jnp.mean(values * values, axis=-1, keepdims=True) + norm_eps) * gain


def swiglu(gate_act, up_act):
    return jax.nn.silu(gate_act) * up_act


def exact(left, right, dims=NN):
    return lax.dot_general(left, right, dims, preferred_element_type=f32)


def select_rows(rows, array, dims=NN):
    picks = rows[:, None] == jnp.arange(array.shape[0], dtype=jnp.int32)[None, :]
    return exact(picks.astype(bf16), array, dims).astype(bf16)


def routing(seq_len, dealt_slot, parts, own_index):
    share = MB_TOK // parts
    count = seq_len.shape[0]
    order = jnp.arange(count, dtype=jnp.int32)
    holder = jnp.sum(jnp.where(dealt_slot[None, :] == order[:, None], order[None, :], 0), axis=1)
    piece = seq_len // parts
    begin = jnp.sum(jnp.where(order[None, :] < order[:, None], piece[None, :], 0), axis=1)
    holds = holder[:, None] == order[None, :]
    slot_len = jnp.sum(jnp.where(holds, seq_len[None, :], 0), axis=1)
    slot_len = slot_len.reshape(parts, MICRO, SEQ_MB)
    slot_given = jnp.sum(jnp.where(holds, begin[None, :], 0), axis=1)
    slot_given = slot_given.reshape(parts, MICRO, SEQ_MB)
    slot_piece = slot_len // parts
    slot_row = jnp.arange(share, dtype=jnp.int32)
    place = jnp.arange(MB_TOK, dtype=jnp.int32)
    source = jnp.arange(parts, dtype=jnp.int32)
    micro = jnp.arange(MICRO, dtype=jnp.int32)
    first = jnp.cumsum(slot_piece, axis=2) - slot_piece
    row = slot_row[None, None, :, None]
    inside = (row >= first[:, :, None, :]) & (row < (first + slot_piece)[:, :, None, :])
    send = jnp.sum(
        jnp.where(inside, slot_given[:, :, None, :] + row - first[:, :, None, :], 0), axis=3
    )
    own_len = lax.dynamic_index_in_dim(slot_len, own_index, 0, keepdims=False)
    own_piece = own_len // parts
    own_first = jnp.cumsum(own_piece, axis=1) - own_piece
    own_start = jnp.cumsum(own_len, axis=1) - own_len
    offset = place[None, :, None] - own_start[:, None, :]
    covered = (offset >= 0) & (offset < own_len[:, None, :])
    per = own_piece[:, None, :]
    flat = (
        offset // per * (MICRO * share)
        + micro[:, None, None] * share
        + own_first[:, None, :]
        + offset % per
    )
    arrange = jnp.sum(jnp.where(covered, flat, 0), axis=2).reshape(-1)
    position = jnp.sum(jnp.where(covered, offset, 0), axis=2).reshape(-1)
    label = jnp.sum(
        jnp.where(covered, jnp.arange(SEQ_MB, dtype=jnp.int32)[None, None, :], 0), axis=2
    ).reshape(-1)
    return send.reshape(-1), arrange, position, label


def gate_tables(gate_in, a_log, dt_bias):
    rate = -jnp.exp(a_log) * jax.nn.softplus(gate_in[:, :H] + dt_bias)
    place = jnp.arange(MB_TOK, dtype=jnp.int32)
    lower = (place[:, None] >= place[None, :]).astype(f32)
    total = jnp.einsum(
        "ij,cjh->cih", lower, rate.reshape(MICRO, MB_TOK, H), precision=lax.Precision.HIGHEST
    ).reshape(ROWS, H)
    return total, jax.nn.sigmoid(gate_in[:, H:])


def gather_full(shard):
    reps = lax.axis_size("dp")
    if shard.shape[0] % (8 * reps) == 0:
        rows = shard.shape[0] // reps
        part = lax.dynamic_slice_in_dim(shard, lax.axis_index("dp") * rows, rows, 0)
        return lax.all_gather(part, ("fsdp", "dp"), axis=0, tiled=True)
    return lax.all_gather(shard, "fsdp", axis=0, tiled=True)


def reduce_grad(grad):
    parts, reps = lax.axis_size("fsdp"), lax.axis_size("dp")
    if grad.shape[0] % (8 * parts * reps) == 0:
        part = lax.psum_scatter(grad, ("fsdp", "dp"), scatter_dimension=0, tiled=True)
        return lax.all_gather(part, "dp", axis=0, tiled=True).astype(f32)
    part = lax.psum_scatter(grad, "fsdp", scatter_dimension=0, tiled=True)
    return lax.psum(part, "dp").astype(f32)


def local(
    tokens,
    cotangent,
    lengths,
    dealing,
    gain_mix,
    w_qkv,
    w_gates,
    w_outgate,
    conv_weight,
    a_log,
    dt_bias,
    out_norm_gain,
    w_out,
    gain_ffn,
    w_gate,
    w_up,
    w_down,
):
    parts = lax.axis_size("fsdp")
    own = lax.axis_index("fsdp")
    width = tokens.shape[2]
    share = MB_TOK // parts
    plane = Plane() if (parts, lax.axis_size("dp")) == (8, 4) else None
    send, arrange, position, label = routing(lengths[0], dealing[0], parts, own)

    def exchange(rows):
        return lax.all_to_all(
            rows.reshape(parts, MICRO * share, width),
            "fsdp",
            split_axis=0,
            concat_axis=0,
            tiled=True,
        ).reshape(ROWS, width)

    def give_back(rows):
        return select_rows(send, exchange(select_rows(arrange, rows, TN)), TN)[None]

    def gram(left, right):
        return exact(left, right, TN).astype(bf16)

    small = (gain_mix, gain_ffn, w_gates, conv_weight.T)
    packed = jnp.concatenate([item.reshape(-1) for item in small])
    extra = -(-packed.size // (8 * width)) * 8
    packed = jnp.pad(packed, (0, extra * width - packed.size)).reshape(1, extra, width)
    rows_x = select_rows(send, tokens[0])
    recv_x = lax.all_to_all(
        jnp.concatenate(
            [
                rows_x.reshape(parts, MICRO * share, width),
                jnp.broadcast_to(packed, (parts, extra, width)),
            ],
            axis=1,
        ),
        "fsdp",
        split_axis=0,
        concat_axis=0,
        tiled=True,
    )
    w_mix = jnp.concatenate([w_qkv, w_outgate], axis=1)
    late = (w_down, w_out, w_gate, w_up)
    if plane:
        units = plane.units()
        widths = (3 * width, 2 * width, w_gate.shape[1], w_up.shape[1])
        mix = Gather(plane, plane.half(w_mix))
        mix.pass_to((1, 0), (0, 0), dz=1)
        far = plane.move(plane.mine(mix.got[0, 0]), dz=2)
        mix.pass_to((0, 1), (0, 0), dx=1)
        mix.share((0, 0))
        quarter = after(late_quarter(*late), mix.got[0, 0])
        recv_x = after(recv_x, far, mix.got[0, 1], mix.got[1, 0], quarter)
        far = after(far, recv_x)
        mix.wait([(0, 1), (1, 0)], recv_x)
        far_y = plane.move(far, dy=1)
        corner = plane.move(far, dz=1)
        mix.pass_to((1, 1), (1, 0), dx=1)
        mix.share((0, 1), (1, 0))
        late_full = lax.all_gather(
            after(quarter, recv_x), ("fsdp", "dp"), axis=0, tiled=True
        )
        recv_x = after(recv_x, mix.from_core[0, 1], mix.from_core[1, 0])
    else:
        full_mix = gather_full(w_mix)
        full_down, full_out, full_gate, full_up = (gather_full(item) for item in late)
    packed = recv_x[:, MICRO * share :].reshape(parts, -1)
    full, start = [], 0
    for item in small:
        piece = packed[:, start : start + item.size]
        full.append(piece.reshape((parts,) + item.shape))
        start += item.size
    full_gain_mix, full_gain_ffn = (item.reshape(-1).astype(f32) for item in full[:2])
    full_gates = full[2].reshape(width, -1)
    taps = jnp.swapaxes(full[3], 0, 1).reshape(TAPS, -1).astype(f32)

    place = arrange + arrange // (MICRO * share) * extra
    local_x = select_rows(place, recv_x.reshape(-1, width))
    inputs_f = local_x.astype(f32)
    normed, mix_back = jax.vjp(rms_scale, inputs_f, full_gain_mix)
    normed_low = normed.astype(bf16)
    if plane:
        far_y = after(far_y, normed_low)
        corner = after(corner, normed_low)
        mix.wait([(1, 1)], normed_low)
        mix.got[2, 0] = plane.join(far, far_y)
        mix.pass_to((2, 1), (2, 0), dx=1)
        corner_y = plane.move(corner, dy=1)
        mix.share((1, 1), (2, 0))
        normed_low = after(normed_low, mix.from_core[1, 1], mix.from_core[2, 0])
    gate_in = exact(normed_low, full_gates)
    (total, strength), gates_back = jax.vjp(gate_tables, gate_in, a_log, dt_bias)
    spread = lambda item: jnp.broadcast_to(item.astype(f32)[:, None], (ROWS, H))
    table = jnp.stack(
        [total, strength, spread(label), spread(position)] + [jnp.zeros((ROWS, H), f32)] * 4
    )
    col = jnp.transpose(table, (2, 1, 0))
    row = jnp.transpose(table, (2, 0, 1))
    gain = out_norm_gain[None, :]
    if plane:
        corner_y = after(corner_y, col, row)
        mix.got[3, 0] = plane.join(corner, corner_y)
        mix.pass_to((3, 1), (3, 0), dx=1)
        mix.share((3, 0))
        mix.wait([(2, 1)], mix.from_core[3, 0])
        mix.share((2, 1))
        mix.wait([(3, 1)], mix.from_core[2, 1])
        mix.share((3, 1))
        mix_blocks = [mix.got[at] for at in BLOCKS] + [mix.from_core[at] for at in BLOCKS]
        projected = project(units, normed_low, mix_blocks, 512)
    else:
        projected = exact(normed_low, full_mix)
    count = H // 2
    firsts = (0, count)
    mixed = [mixer_forward(projected, col, row, taps, gain, firsts[0], count)]
    mixed.append(mixer_forward(projected, col, row, taps, gain, firsts[1], count))
    given_cot = after(cotangent[0], mixed[0][0])
    recv_cot = exchange(select_rows(send, given_cot))
    if plane:
        residual, ffn_turned, gate_act, up_act, hidden_turned, result = ffn_forward(
            mixed[0][0], mixed[1][0], local_x, full_gain_ffn[None, :], late_full
        )
        local_cot = select_rows(arrange, after(recv_cot, result))
        down = Reduce(
            plane, gram_blocks(units, hidden_turned, [local_cot], 1024, widths[0])
        )
        rows_out = select_rows(arrange, after(result, down.send), TN)
        recv_out = exchange(rows_out)
        sent = down.start(rows_out)
        gate_low, up_low, grad_residual, mix_low, grad_gated, grad_gain_ffn = ffn_backward(
            after(local_cot, sent), residual, full_gain_ffn[None, :], gate_act, up_act,
            late_full,
        )
        sent = down.turn(grad_gated, recv_out)
        gated_t = jnp.concatenate([part[1] for part in mixed], axis=0)
        wide = widths[1] + widths[2]
        sums = gram_blocks(units, gated_t, [after(mix_low, sent)], 1024, wide)
        sums = gram_blocks(units, ffn_turned, [gate_low], FTILE, wide, widths[1], sums)
        out_gate_sums = Reduce(plane, sums)
        up = Reduce(
            plane,
            gram_blocks(
                units, ffn_turned, [after(up_low, out_gate_sums.send)], FTILE, widths[3]
            ),
            split=True,
        )
        sent = out_gate_sums.start(up.send)
        sent = up.start(sent)
    else:
        local_cot = select_rows(arrange, recv_cot)
        gated_low = jnp.concatenate([part[0] for part in mixed], axis=1)
        residual = inputs_f + exact(gated_low, full_out)
        ffn_normed, ffn_back = jax.vjp(rms_scale, residual, full_gain_ffn)
        ffn_low = ffn_normed.astype(bf16)
        gate_act = exact(ffn_low, full_gate)
        up_act = exact(ffn_low, full_up)
        hidden, act_back = jax.vjp(swiglu, gate_act, up_act)
        hidden_low = hidden.astype(bf16)
        result = (residual + exact(hidden_low, full_down)).astype(bf16)
        output = give_back(result)
        grad_gate_act, grad_up_act = act_back(exact(local_cot, full_down, NT))
        gate_low, up_low = grad_gate_act.astype(bf16), grad_up_act.astype(bf16)
        grad_part, grad_gain_ffn = ffn_back(
            exact(gate_low, full_gate, NT) + exact(up_low, full_up, NT)
        )
        grad_residual = local_cot.astype(f32) + grad_part
        mix_low = grad_residual.astype(bf16)
        grad_gated = exact(mix_low, full_out, NT)
        late_grads = [
            reduce_grad(gram(left, right))
            for left, right in (
                (hidden_low, local_cot), (gated_low, mix_low), (ffn_low, gate_low),
                (ffn_low, up_low),
            )
        ]
    backs = []
    for part, first in zip(mixed, firsts):
        grad = after(grad_gated, sent) if plane else grad_gated
        backs.append(
            mixer_backward(projected, grad, col, row, taps, gain, part[2], part[3], first)
        )
        if plane and not first:
            sent = down.along(backs[0][0])
    rights = [back[i] for i in range(4) for back in backs]
    dtap_q, dtap_k, dtap_v = (
        jnp.concatenate([back[i] for back in backs], axis=1) for i in (4, 5, 6)
    )
    dgain, dcol, drow = (jnp.concatenate([back[i] for back in backs]) for i in (7, 8, 9))
    if plane:
        left = normed_low.T
        sent = out_gate_sums.turn(backs[1][0])
        sent = up.beside(sent)
        rights[4] = after(rights[4], sent)
        vo = Reduce(plane, gram_blocks(units, left, rights[4:], 512, 2 * H * DV), split=True)
        rights[0] = after(rights[0], vo.send)
        qk = Reduce(plane, gram_blocks(units, left, rights[:4], 512, 2 * H * DK))
        sent = vo.start(qk.send)
        sent = out_gate_sums.along(sent)
        sent = qk.start(sent)
        sent = up.turn(sent)
        rights[0] = after(rights[0], sent)
        grad_normed = back_project(units, rights, mix_blocks, width, 512)
        sent = qk.turn(grad_normed)
        sent = up.along(sent)
        sent = down.across(sent)
        sent = out_gate_sums.across(sent)
        sent = vo.beside(sent)
    else:
        low = jnp.concatenate(rights, axis=1)
        grad_mix = reduce_grad(gram(normed_low, low))
        grad_normed = exact(low, full_mix, NT)
    grad_conv = jnp.concatenate([dtap_q, dtap_k, dtap_v], axis=1).reshape(TAPS, parts, -1)
    grad_conv = jnp.swapaxes(grad_conv, 0, 1)
    grad_out_gain = jnp.sum(dgain[:, 0], axis=0)
    grad_strength = drow[:, 0].T
    grad_total = dcol[:, :, 0].T - strength * grad_strength
    grad_gate_in, grad_a_log, grad_dt_bias = gates_back((grad_total, grad_strength))
    gate_in_low = grad_gate_in.astype(bf16)
    grad_gates = exact(normed_low, gate_in_low, TN)
    grad_normed = grad_normed + exact(gate_in_low, full_gates, NT)
    grad_part, grad_gain_mix = mix_back(grad_normed)
    grad_inputs = (grad_residual + grad_part).astype(bf16)
    if plane:
        rows_in = select_rows(arrange, after(grad_inputs, sent), TN)
        recv_in = exchange(rows_in)
        sent = qk.along(rows_in)
        sent = up.across(sent)
        sent = down.close(sent)
        output = select_rows(send, after(recv_out, sent), TN)[None]
    else:
        input_grad = give_back(grad_inputs)

    small_grads = (grad_gain_mix, grad_gain_ffn, grad_gates, grad_conv)
    alone = (grad_a_log, grad_dt_bias, grad_out_gain)
    sums = jnp.concatenate(
        [item.reshape(parts, -1) for item in small_grads]
        + [jnp.broadcast_to(jnp.concatenate(alone)[None], (parts, 2 * H + DV))],
        axis=1,
    )
    if plane:
        def add_small(sums, step, *others):
            pairs = [(i, i ^ step) for i in range(32)]
            return sums + lax.ppermute(after(sums, *others), ("fsdp", "dp"), pairs)

        sums = add_small(sums, 1, sent)
        sent = out_gate_sums.close(sent)
        sent = vo.turn(sent, sums)
        sums = add_small(sums, 4, sent)
        sent = qk.across(sent)
        sent = up.close(sent)
        sent = vo.along(sent, sums)
        sums = add_small(sums, 2, sent)
        sent = qk.close(sent)
        sent = vo.across(sent, sums)
        sums = add_small(sums, 8, sent)
        input_grad = select_rows(send, after(recv_in, sent), TN)[None]
        sent = vo.close(sent, sums)
        sums = add_small(sums, 16, sent)
        out_gate_halves = out_gate_sums.halves()
        cut = widths[1]

        def whole(halves, rows, columns):
            return jnp.concatenate(
                [rows_of(part, rows // 2, columns) for part in halves], axis=0
            ).astype(f32)

        late_grads = (
            whole(down.halves(), w_down.shape[0], width),
            whole([part[:, :cut] for part in out_gate_halves], w_out.shape[0], width),
            jnp.concatenate([part[:, cut:] for part in out_gate_halves], axis=0).astype(f32),
            jnp.concatenate(up.halves(), axis=0).astype(f32),
        )
        qk_grad, vo_grad = (
            jnp.concatenate(item.halves(), axis=0).astype(f32) for item in (qk, vo)
        )
        grad_qkv = jnp.concatenate([qk_grad, vo_grad[:, : H * DV]], axis=1)
        grad_outgate = vo_grad[:, H * DV :]
    else:
        sums = lax.psum(sums, ("fsdp", "dp"))
        grad_qkv, grad_outgate = grad_mix[:, : w_qkv.shape[1]], grad_mix[:, w_qkv.shape[1] :]
    sums = lax.dynamic_index_in_dim(sums, own, 0, keepdims=False)
    ready, start = [], 0
    for item in small + alone:
        ready.append(sums[start : start + item.size].reshape(item.shape))
        start += item.size
    return (
        output,
        input_grad,
        ready[0],
        grad_qkv,
        ready[2],
        grad_outgate,
        ready[3].T,
        ready[4],
        ready[5],
        ready[6],
        late_grads[1],
        ready[1],
        late_grads[2],
        late_grads[3],
        late_grads[0],
    )


def solution(mesh):
    in_specs = (
        P("dp", "fsdp", None),
        P("dp", "fsdp", None),
        P("dp", None),
        P("dp", None),
        P("fsdp"),
        P("fsdp", None),
        P("fsdp", None),
        P("fsdp", None),
        P("fsdp", None),
        P(),
        P(),
        P(),
        P("fsdp", None),
        P("fsdp"),
        P("fsdp", None),
        P("fsdp", None),
        P("fsdp", None),
    )
    out_specs = (
        P("dp", "fsdp", None),
        P("dp", "fsdp", None),
        P("fsdp"),
        P("fsdp", None),
        P("fsdp", None),
        P("fsdp", None),
        P("fsdp", None),
        P(),
        P(),
        P(),
        P("fsdp", None),
        P("fsdp"),
        P("fsdp", None),
        P("fsdp", None),
        P("fsdp", None),
    )
    return jax.shard_map(local, mesh=mesh, in_specs=in_specs, out_specs=out_specs, check_vma=False)
```
